32 devices in a mesh: ctx: 8 (over z, core), inner: 4 (over y, x).
Axes of the slice: x: 2, y: 2, z: 4, core: 2. Of those that a mesh axis runs over, the one named last changes fastest.
Arguments:
- tokens: bfloat16 [4096, 2048], P(('ctx', 'inner')), may hold values from -6 to 6
- project_weight: bfloat16 [2048, 2, 4096], P('ctx', None, 'inner'), may hold values from -0.125 to 0.125
- state_weight: bfloat16 [2048, 2, 512], P('ctx', None, 'inner'), may hold values from -0.125 to 0.125
- step_weight: bfloat16 [2048, 64], P('ctx', 'inner'), may hold values from -0.125 to 0.125
- mixer_taps: float32 [5, 4096], P(None, 'inner'), may hold values from -2.5 to 2.5
- state_taps: float32 [5, 2, 512], replicated, may hold values from -2.5 to 2.5
- step_bias: float32 [64], P('inner'), may hold values from -4.6 to -2.3
- decay_log: float32 [64], P('inner'), may hold values from -13 to 0.5, as said below
- norm_gain: float32 [4096], replicated, may hold values from 0.1 to 1.9
Outputs:
- mixed_output: bfloat16 [4096, 4096], P(('ctx', 'inner'))
The draws below stay inside these ranges and needn't reach their ends.
Inputs may be any that keep to these rules, and one draw needn't show every extreme that they name: `decay_log`: one value a head.
All inputs are finite; a program needn't handle non-finite values.
Results may differ from the reference program's by a relative error of at most 0.0075.
Values may be sent and summed in bfloat16 or wider, within the bound.
No kernel may reach another device: no remote copies, remote signals or barrier semaphores. Data moves between devices by JAX's collectives and lax.ppermute only.
A program may use at most 64 MiB of HBM per device.

```python
import jax
import jax.numpy as jnp
from jax import lax

D = 2048
H = 64
P_SIZE = 64
N = 128
G = 4
CONV = 4
SPAN = 128
E = 4096
TOKENS = 4096


def draw_decay_log(key, part):
    first_key = jax.random.fold_in(key, 0)
    return jax.random.uniform(first_key, (H,), jnp.float32, -13.0, 0.5)


def block_scale(key, extent, cuts, least, high):
    gain = 1.0
    for position, shards_of in cuts:
        draws = jax.random.uniform(jax.random.fold_in(jax.random.fold_in(key, 6), position), (shards_of,), jnp.float32, least / len(cuts), high / len(cuts))
        gain = gain * jnp.repeat(jnp.exp(draws), extent[position] // shards_of).reshape((-1,) + (1,) * (len(extent) - 1 - position))
    return gain


def noise(rng, shape, scale, most, cuts=(), held_as=jnp.bfloat16):
    factor_of = block_scale(rng, shape, cuts, -0.22, 0.18) if cuts else 1.0
    entries = jax.random.normal(rng, shape, jnp.float32) * scale * factor_of
    return jnp.minimum(jnp.maximum(entries, -most), most).astype(held_as)


def setup_inputs(seed: int = 0) -> dict:
    key_list = jax.random.split(jax.random.key(seed), 10)
    tokens = noise(key_list[0], (TOKENS, D), 1.0, 6.0, ((0, 32),))
    project_weight = noise(key_list[1], (D, 2, E), D ** -0.5, 0.125, ((0, 8), (2, 4)))
    state_weight = noise(key_list[2], (D, 2, G * N), D ** -0.5, 0.125, ((0, 8), (2, 4)))
    step_weight = noise(key_list[3], (D, H), D ** -0.5, 0.125, ((0, 8), (1, 4)))
    mixer_taps = noise(key_list[4], (CONV + 1, E), 0.5, 2.5, ((1, 4),), jnp.float32)
    state_taps = noise(key_list[5], (CONV + 1, 2, G * N), 0.5, 2.5, (), jnp.float32)
    step_bias = jnp.clip(-4.6 + 2.3 * jax.random.uniform(key_list[6], (H,), jnp.float32) ** block_scale(key_list[6], (H,), ((0, 4),), -0.2, 0.2), -4.6, -2.3)
    decay_log = draw_decay_log(jax.random.fold_in(key_list[9], 71), 0)
    norm_gain = jnp.clip(1.0 + 0.18 * jax.random.normal(key_list[8], (E,), jnp.float32), 0.1, 1.9)
    return dict(tokens=tokens, project_weight=project_weight, state_weight=state_weight, step_weight=step_weight, mixer_taps=mixer_taps, state_taps=state_taps, step_bias=step_bias, decay_log=decay_log, norm_gain=norm_gain)


EPSILON = 1e-05

def reference(tokens, project_weight, state_weight, step_weight, mixer_taps, state_taps, step_bias, decay_log, norm_gain):
    length_all = tokens.shape[0]
    blocks = length_all // SPAN
    channels = H * P_SIZE
    group_cols = G * N
    heads_group = H // G
    flat_project = project_weight.reshape(D, 2 * channels)
    flat_state = state_weight.reshape(D, 2 * group_cols)
    taps_all = jnp.concatenate([mixer_taps, state_taps.reshape(CONV + 1, 2 * group_cols)], axis=1)
    rates = -jnp.exp(decay_log)
    lower = jnp.tril(jnp.ones((SPAN, SPAN), dtype=bool))

    def advance(carry, rows):
        state, rim_rows = carry
        projected = jnp.dot(rows, flat_project, preferred_element_type=jnp.float32).astype(jnp.bfloat16)
        state_pre = jnp.dot(rows, flat_state, preferred_element_type=jnp.float32).astype(jnp.bfloat16)
        step_raw = jnp.dot(rows, step_weight, preferred_element_type=jnp.float32).astype(jnp.bfloat16)
        gate_values = projected[:, :channels]
        current = jnp.concatenate([projected[:, channels:], state_pre], axis=1)
        extended = jnp.concatenate([rim_rows, current], axis=0)
        mixed = jnp.broadcast_to(taps_all[CONV], current.shape).astype(jnp.float32)
        for offset in range(CONV):
            mixed = mixed + taps_all[offset] * extended[offset:offset + SPAN].astype(jnp.float32)
        active = jax.nn.silu(mixed).astype(jnp.bfloat16)
        x_vals = active[:, :channels].reshape(SPAN, H, P_SIZE).astype(jnp.float32)
        b_vals = active[:, channels:channels + group_cols].reshape(SPAN, N, G).transpose(0, 2, 1).astype(jnp.float32)
        c_vals = active[:, channels + group_cols:].reshape(SPAN, N, G).transpose(0, 2, 1).astype(jnp.float32)
        step_size = jax.nn.softplus(step_raw.astype(jnp.float32) + step_bias)
        cumul = jnp.cumsum(step_size * rates, axis=0)
        scores = jnp.einsum('tgn,sgn->gts', c_vals, b_vals, precision=lax.Precision.HIGHEST)
        scores = jnp.repeat(scores, heads_group, axis=0)
        cumul_heads = cumul.T
        spacing = jnp.where(lower[None], cumul_heads[:, :, None] - cumul_heads[:, None, :], -jnp.inf)
        mixing = (scores * jnp.exp(spacing) * step_size.T[:, None, :]).astype(jnp.bfloat16)
        diagonal = jnp.einsum('hts,shp->thp', mixing.astype(jnp.float32), x_vals, precision=lax.Precision.HIGHEST)
        ending = cumul[-1]
        to_end = jnp.exp(ending[None] - cumul) * step_size
        b_heads = jnp.repeat(b_vals, heads_group, axis=1)
        weighted_b = lax.optimization_barrier((b_heads * to_end[:, :, None]).astype(jnp.bfloat16)).astype(jnp.float32)
        c_heads = jnp.repeat(c_vals, heads_group, axis=1) * jnp.exp(cumul)[:, :, None]
        weighted_c = lax.optimization_barrier(c_heads.astype(jnp.bfloat16)).astype(jnp.float32)
        fresh = jnp.einsum('shn,shp->hnp', weighted_b, x_vals, precision=lax.Precision.HIGHEST)
        offdiag = jnp.einsum('thn,hnp->thp', weighted_c, state, precision=lax.Precision.HIGHEST)
        state_next = jnp.exp(ending)[:, None, None] * state + fresh
        outputs = (diagonal + offdiag).reshape(SPAN, channels)
        gated = (outputs * jax.nn.silu(gate_values.astype(jnp.float32))).astype(jnp.bfloat16)
        grouped = gated.astype(jnp.float32).reshape(SPAN, G, channels // G)
        power = lax.optimization_barrier(jnp.mean(grouped * grouped, axis=-1, keepdims=True))
        normed = (grouped * lax.rsqrt(power + EPSILON)).reshape(SPAN, channels) * norm_gain
        return ((state_next, extended[SPAN:]), normed.astype(jnp.bfloat16))
    start_carry = (jnp.zeros((H, N, P_SIZE), jnp.float32), jnp.zeros((CONV - 1, channels + 2 * group_cols), jnp.bfloat16))
    _, results = lax.scan(advance, start_carry, tokens.reshape(blocks, SPAN, D))
    return results.reshape(length_all, channels)
```

```python
import jax
import jax.numpy as jnp
from jax import lax
from jax.experimental import pallas as pl
from jax.experimental.pallas import tpu as pltpu
from jax.sharding import PartitionSpec as P

H = 64
P_SIZE = 64
N = 128
G = 4
CONV = 4
SPAN = 128
TEAM = 4
HALO = 16
LANES = 128
PAD = 8

EPSILON = 1e-05


def swapped(x, axis, mask):
    pairs = [(i, i ^ mask) for i in range(lax.axis_size(axis))]
    return lax.ppermute(x, axis, pairs)


def pick(values, index, axis):
    return lax.dynamic_index_in_dim(values, index, axis, keepdims=False)


def inner_blocks(block, core, inner_count, ctx_count):
    if inner_count != 4:
        got = [block]
        step = 1
        while step < inner_count:
            got = got + [swapped(b, "inner", step) for b in got]
            step *= 2
        return got
    near_x = swapped(block, "inner", 1)
    near_y = swapped(block, "inner", 2)
    pairs = []
    for c in range(ctx_count):
        for i in range(inner_count):
            pairs.append((c * inner_count + i, c * inner_count + (i ^ (1 if c % 2 else 2))))
    onward = jnp.where(core == 0, near_x, near_y)
    far = lax.ppermute(onward, ("ctx", "inner"), pairs)
    return [block, near_x, near_y, far]


def gathered_rows(piece_of, z_count):
    return [piece_of(d) if d == 0 else swapped(piece_of(d), "ctx", 2 * d) for d in range(z_count)]


ANY = pl.BlockSpec(memory_space=pl.ANY)
VMEM = pl.BlockSpec(memory_space=pltpu.VMEM)
SMEM = pl.BlockSpec(memory_space=pltpu.SMEM)
F32 = jnp.float32
BF16 = jnp.bfloat16


def fetch_weights(place, pieces, scratch, sems, column=0):
    z_id, core = place[2], place[3]
    half = pieces[0].shape[0] // 2
    width = pieces[0].shape[1]
    copies = []
    for d, piece in enumerate(pieces):
        for m in range(2):
            row = pl.multiple_of((2 * (z_id ^ d) + (core ^ m)) * half, half)
            copies.append(
                pltpu.make_async_copy(
                    piece.at[pl.ds(m * half, half)],
                    scratch.at[pl.ds(row, half), pl.ds(column, width)],
                    sems.at[2 * d + m],
                )
            )
    for copy in copies:
        copy.start()
    return copies


def fetch_blocks(place, blocks, scratch, sems, inner_count, offset):
    inner_id = place[1]
    rows = blocks[0].shape[0]
    copies = []
    for d, block in enumerate(blocks):
        j, di = d // inner_count, d % inner_count
        row = pl.multiple_of(offset + j * inner_count * rows + (inner_id ^ di) * rows, HALO)
        copies.append(pltpu.make_async_copy(block, scratch.at[pl.ds(row, rows)], sems.at[d]))
    for copy in copies:
        copy.start()
    return copies


def wide_dot(a, b):
    return jnp.dot(a, b, preferred_element_type=F32)


def exact_dot(a, b, dims):
    return lax.dot_general(a, b, (dims, ((), ())), precision=lax.Precision.HIGHEST, preferred_element_type=F32)


def convolved(pre, taps, block):
    window = pre[pl.ds(pl.multiple_of(block * SPAN, SPAN), SPAN + HALO), :].astype(F32)
    start = HALO - (CONV - 1)
    mixed = taps[CONV : CONV + 1, :] + taps[0:1, :] * window[start : start + SPAN]
    for k in range(1, CONV):
        mixed = mixed + taps[k : k + 1, :] * window[start + k : start + k + SPAN]
    return mixed / (1.0 + jnp.exp(-mixed))


def spread(heads, width):
    row = lax.broadcasted_iota(jnp.int32, (PAD, width), 0)
    column = lax.broadcasted_iota(jnp.int32, (PAD, width), 1)
    return (column // P_SIZE == row).astype(F32)


def projected(place, blocks, halo, pieces, tok, weight, sems, wsems, inner_count, keep, extra=()):
    waits = fetch_weights(place, pieces, weight, wsems)
    for index, (more, column) in enumerate(extra):
        waits = waits + fetch_weights(place, more, weight, wsems.at[pl.ds((index + 1) * 2 * len(pieces), 2 * len(pieces))], column)
    offset = 0
    if halo is not None:
        offset = HALO
        top = pltpu.make_async_copy(halo, tok.at[pl.ds(0, HALO)], sems.at[len(blocks)])
        top.start()
        waits = waits + [top]
    copies = fetch_blocks(place, blocks, tok, sems, inner_count, offset)
    for copy in waits:
        copy.wait()
    span = inner_count * blocks[0].shape[0]
    for j in range(TEAM):
        for di in range(inner_count):
            copies[j * inner_count + di].wait()
        first = 0 if j == 0 else offset + j * span
        size = span + (offset if j == 0 else 0)
        keep(wide_dot(tok[pl.ds(first, size), :], weight[...]), j)


def state_kernel(inner_count, counts, place, taps, bias, rate, *refs):
    n_blocks, n_pieces = counts
    blocks, refs = refs[:n_blocks], refs[n_blocks:]
    halo, refs = refs[0], refs[1:]
    pieces, refs = refs[:n_pieces], refs[n_pieces:]
    steps, refs = refs[:n_pieces], refs[n_pieces:]
    half_out, step_out, cum_out, tok, weight, pre, sems, wsems = refs
    span = inner_count * blocks[0].shape[0]
    quarter = place[0]

    def keep(result, j):
        if j == 0:
            pre[pl.ds(0, HALO), :] = result[:HALO, :N].astype(BF16)
            result = result[HALO:]
        whose = quarter ^ j
        pre[pl.ds(pl.multiple_of(HALO + whose * span, HALO), span), :] = result[:, :N].astype(BF16)
        raw = result[:, N:].astype(BF16).astype(F32)
        for b in range(span // SPAN):
            turned = raw[b * SPAN : (b + 1) * SPAN].T
            step_out[whose * (span // SPAN) + b] = turned[:PAD]

    projected(place, blocks, halo, pieces, tok, weight, sems, wsems, inner_count, keep, ((steps, N),))

    total = step_out.shape[0] * PAD
    raw = step_out[...] + bias[...][None]
    step = jnp.maximum(raw, 0.0) + jnp.log1p(jnp.exp(-jnp.abs(raw)))
    step_out[...] = step
    logdec = (step * rate[...][None]).reshape(total, SPAN)
    row = lax.broadcasted_iota(jnp.int32, (SPAN, SPAN), 0)
    column = lax.broadcasted_iota(jnp.int32, (SPAN, SPAN), 1)
    upper = (row <= column).astype(F32)
    cum_out[...] = exact_dot(logdec, upper, ((1,), (0,))).reshape(step_out.shape)

    def one(p, _):
        half_out[pl.ds(pl.multiple_of(p * SPAN, SPAN), SPAN), :] = convolved(pre, taps, p).astype(BF16)
        return 0

    lax.fori_loop(0, step_out.shape[0], one, 0, unroll=2)


def mixer_kernel(inner_count, counts, place, taps, b_vals, step, cum, *refs):
    n_blocks, n_pieces = counts
    blocks, refs = refs[:n_blocks], refs[n_blocks:]
    halo, refs = refs[0], refs[1:]
    pieces, refs = refs[:n_pieces], refs[n_pieces:]
    x_out, states_out, last_out, through_out, tok, weight, pre, sems, wsems = refs
    span = inner_count * blocks[0].shape[0]
    quarter = place[0]
    width = x_out.shape[1]

    def keep(result, j):
        if j == 0:
            pre[pl.ds(0, HALO), :] = result[:HALO].astype(BF16)
            result = result[HALO:]
        whose = quarter ^ j
        pre[pl.ds(pl.multiple_of(HALO + whose * span, HALO), span), :] = result.astype(BF16)

    projected(place, blocks, halo, pieces, tok, weight, sems, wsems, inner_count, keep)
    heads = spread(width // P_SIZE, width)

    def one(p, carry):
        state, log_sum = carry
        rows = pl.ds(pl.multiple_of(p * SPAN, SPAN), SPAN)
        x = convolved(pre, taps, p).astype(BF16)
        x_out[rows, :] = x
        states_out[p] = state
        cum_p = cum[p]
        ends = cum_p[:, SPAN - 1 :]
        to_end = jnp.exp(ends - cum_p) * step[p]
        scaled = (x.astype(F32) * exact_dot(to_end, heads, ((0,), (0,)))).astype(BF16)
        fresh = lax.dot_general(
            b_vals[rows, :], scaled, (((0,), (0,)), ((), ())), preferred_element_type=F32
        )
        end_row = jnp.sum(ends * heads, axis=0, keepdims=True)
        return jnp.exp(end_row) * state + fresh, log_sum + end_row

    state, log_sum = lax.fori_loop(
        0, step.shape[0], one, (jnp.zeros((N, width), F32), jnp.zeros((1, width), F32)), unroll=2
    )
    last_out[...] = state.astype(BF16)
    through_out[...] = jnp.broadcast_to(jnp.exp(log_sum), through_out.shape)


def gate_kernel(inner_count, counts, place, *refs):
    n_blocks, n_pieces = counts
    blocks, refs = refs[:n_blocks], refs[n_blocks:]
    pieces, refs = refs[:n_pieces], refs[n_pieces:]
    gate_out, tok, weight, sems, wsems = refs
    span = inner_count * blocks[0].shape[0]
    quarter = place[0]

    def keep(result, j):
        gate_out[pl.ds(pl.multiple_of((quarter ^ j) * span, span), span), :] = result.astype(BF16)

    projected(place, blocks, None, pieces, tok, weight, sems, wsems, inner_count, keep)


def scan_kernel(place, b_core, c_core, x_vals, gate, step, cum, states, prior, gated_out):
    width = x_vals.shape[1]
    heads_mine = width // P_SIZE
    heads = spread(heads_mine, width)
    lane = lax.broadcasted_iota(jnp.int32, (SPAN, width), 1) // P_SIZE
    row = lax.broadcasted_iota(jnp.int32, (SPAN, SPAN), 0)
    column = lax.broadcasted_iota(jnp.int32, (SPAN, SPAN), 1)
    lower = column <= row
    entering = prior[...].astype(F32)

    def one(p, before):
        rows = pl.ds(pl.multiple_of(p * SPAN, SPAN), SPAN)
        c = c_core[rows, :]
        x = x_vals[rows, :]
        cum_p = cum[p]
        step_p = step[p]
        scores = lax.dot_general(
            c, b_core[rows, :], (((1,), (1,)), ((), ())), preferred_element_type=F32
        )
        cum_t = cum_p.T
        mixes = []
        parts = []
        for h in range(heads_mine):
            spacing = jnp.where(lower, cum_t[:, h : h + 1] - cum_p[h : h + 1, :], -jnp.inf)
            mixes.append((scores * jnp.exp(spacing) * step_p[h : h + 1, :]).astype(BF16))
            parts.append(jnp.where(lane == h, x, jnp.zeros_like(x)))
        diagonal = wide_dot(jnp.concatenate(mixes, axis=1), jnp.concatenate(parts, axis=0))
        state = states[p] + jnp.exp(before) * entering
        decay = exact_dot(jnp.exp(cum_p), heads, ((0,), (0,)))
        y = diagonal + decay * wide_dot(c, state.astype(BF16))
        g = gate[rows, :].astype(F32)
        gated_out[rows, :] = (y * (g / (1.0 + jnp.exp(-g)))).astype(BF16)
        return before + jnp.sum(cum_p[:, SPAN - 1 :] * heads, axis=0, keepdims=True)

    lax.fori_loop(0, step.shape[0], one, jnp.zeros((1, width), F32), unroll=2)


def norm_kernel(inner_count, parts, gain, out):
    width = parts.shape[2]
    group_width = H * P_SIZE // G
    for g in range(G):
        members = []
        power = 0.0
        for c in range(g * group_width, (g + 1) * group_width, width):
            index = c // width
            i, k = index // TEAM, index % TEAM
            wide = parts[k * inner_count + i].astype(F32)
            members.append((c, wide))
            power = power + jnp.sum(wide * wide, axis=1, keepdims=True)
        scale = lax.rsqrt(power / group_width + EPSILON)
        for c, wide in members:
            out[:, c : c + width] = (wide * scale * gain[:, c : c + width]).astype(BF16)


def on_device(
    tokens,
    project_weight,
    state_weight,
    step_weight,
    mixer_taps,
    state_taps,
    step_bias,
    decay_log,
    norm_gain,
):
    ctx_count = lax.axis_size("ctx")
    inner_count = lax.axis_size("inner")
    ctx_id = lax.axis_index("ctx")
    inner_id = lax.axis_index("inner")
    core = ctx_id % 2
    z_id = ctx_id // 2
    z_count = ctx_count // 2
    side = z_id % 2
    quarter = ctx_id % TEAM
    members = TEAM * inner_count
    place = jnp.stack([quarter, inner_id, z_id, core]).astype(jnp.int32)

    rows_here, _, width_here = project_weight.shape
    row_count, model_width = tokens.shape
    heads_here = step_weight.shape[1]
    heads_mine = heads_here // TEAM
    width_mine = width_here // TEAM
    per_group = H // G
    group = inner_id * heads_here // per_group
    total = members * row_count
    count = total // SPAN
    chip_rows = 2 * rows_here

    partner = swapped(tokens, "ctx", 2)
    near = inner_blocks(tokens, core, inner_count, ctx_count)
    beyond = inner_blocks(partner, core, inner_count, ctx_count)
    blocks = (
        near
        + [swapped(b, "ctx", 1) for b in near]
        + beyond
        + [swapped(b, "ctx", 1) for b in beyond]
    )
    tail = pick(
        jnp.stack([b[-HALO:] for b in near], axis=0), inner_id ^ (inner_count - 1), 0
    )
    halo = jnp.zeros_like(tail)
    for k in range(TEAM):
        pairs = [(c - 1, c + k) for c in range(TEAM, ctx_count, TEAM)]
        halo = halo + lax.ppermute(tail, "ctx", pairs)

    slice_n = state_weight.shape[2] // G
    by_group = state_weight.reshape(rows_here, 2, slice_n, G)
    to_each = jnp.stack(
        [by_group[..., (j * heads_here) // per_group] for j in range(inner_count)], axis=0
    )
    state_rows = lax.all_to_all(to_each, "inner", 0, 0, tiled=True)
    state_rows = state_rows.reshape(inner_count, rows_here, 2, slice_n)
    state_rows = state_rows.transpose(2, 1, 0, 3).reshape(2, rows_here, N)

    split = project_weight.reshape(rows_here, 2, 2, 2, width_mine)
    step_split = step_weight.reshape(rows_here, 2, 2, heads_mine)

    def by_core(values, axis):
        mine = pick(values, core, axis)
        other = swapped(pick(values, 1 - core, axis), "ctx", 1)
        return jnp.concatenate([mine, other], axis=0)

    chip_project = by_core(split, 3)
    chip_step = by_core(step_split, 2)
    chip_state = by_core(state_rows, 0)

    def side_of(values, d, axis):
        return pick(values, side ^ (d % 2), axis)

    pack = heads_mine * chip_rows // LANES

    def state_payload(d):
        packed = side_of(chip_step, d, 1).T.reshape(pack, LANES)
        return jnp.concatenate([chip_state, packed], axis=0)

    state_pieces = gathered_rows(state_payload, z_count)
    x_pieces = gathered_rows(lambda d: side_of(chip_project[:, 1], d, 1), z_count)
    gate_pieces = gathered_rows(lambda d: side_of(chip_project[:, 0], d, 1), z_count)
    packed = jnp.stack([p[chip_rows:] for p in state_pieces], axis=0)
    packed = packed.reshape(z_count, heads_mine, chip_rows).transpose(0, 2, 1)
    packed = jnp.pad(packed, ((0, 0), (0, 0), (0, LANES - heads_mine)))
    step_pieces = [packed[d] for d in range(z_count)]
    state_pieces = [p[:chip_rows] for p in state_pieces]

    def fill(values, rows):
        return jnp.pad(values, ((0, rows - values.shape[0]),) + ((0, 0),) * (values.ndim - 1))

    taps_group = pick(state_taps.reshape(CONV + 1, 2, N, G), group, 3)
    taps_state = fill(pick(taps_group, core, 1), PAD)
    taps_mine = fill(lax.dynamic_slice_in_dim(mixer_taps, quarter * width_mine, width_mine, 1), PAD)

    def by_head(values):
        mine = lax.dynamic_slice_in_dim(values, quarter * heads_mine, heads_mine, 0)
        return jnp.broadcast_to(fill(mine, PAD)[:, None], (PAD, SPAN))

    bias_mine = by_head(step_bias)
    rate_mine = by_head(-jnp.exp(decay_log))

    def sds(shape, dtype):
        return jax.ShapeDtypeStruct(shape, dtype)

    limit = pltpu.CompilerParams(vmem_limit_bytes=60 * 1024 * 1024)
    counts = (members, z_count)

    def scratch(width, halo_rows, pre_width):
        made = [pltpu.VMEM((halo_rows + total, model_width), BF16), pltpu.VMEM((model_width, width), BF16)]
        if pre_width:
            made.append(pltpu.VMEM((HALO + total, pre_width), BF16))
        copies = 2 * z_count * (2 if pre_width == N and width == 2 * N else 1)
        return made + [pltpu.SemaphoreType.DMA((members + 1,)), pltpu.SemaphoreType.DMA((2 * copies,))]

    any_of = lambda values: [ANY] * len(values)
    half_vals, step, cum = pl.pallas_call(
        lambda *refs: state_kernel(inner_count, counts, *refs),
        in_specs=[SMEM, VMEM, VMEM, VMEM] + any_of(blocks) + [ANY] + any_of(state_pieces) + any_of(step_pieces),
        out_specs=[VMEM, VMEM, VMEM],
        out_shape=[sds((total, N), BF16), sds((count, PAD, SPAN), F32), sds((count, PAD, SPAN), F32)],
        scratch_shapes=scratch(N + LANES, HALO, N),
        compiler_params=limit,
        name="state",
    )(place, taps_state, bias_mine, rate_mine, *blocks, halo, *state_pieces, *step_pieces)
    other_half = swapped(half_vals, "ctx", 1)
    b_vals = jnp.where(core == 0, half_vals, other_half)
    c_vals = jnp.where(core == 0, other_half, half_vals)

    x_vals, states, last_state, through = pl.pallas_call(
        lambda *refs: mixer_kernel(inner_count, counts, *refs),
        in_specs=[SMEM, VMEM, VMEM, VMEM, VMEM] + any_of(blocks) + [ANY] + any_of(x_pieces),
        out_specs=[VMEM, VMEM, VMEM, VMEM],
        out_shape=[
            sds((total, width_mine), BF16),
            sds((count, N, width_mine), F32),
            sds((N, width_mine), BF16),
            sds((PAD, width_mine), F32),
        ],
        scratch_shapes=scratch(width_mine, HALO, width_mine),
        compiler_params=limit,
        name="mixer",
    )(place, taps_mine, b_vals, step, cum, *blocks, halo, *x_pieces)

    hops = ctx_count // TEAM - 1
    pairs = [(c, c + TEAM) for c in range(ctx_count - TEAM)]
    prior = jnp.zeros_like(last_state)
    for hop in range(hops):
        sent = last_state
        if hop:
            sent = (through[:1] * prior.astype(F32) + last_state.astype(F32)).astype(BF16)
        prior = lax.ppermute(sent, "ctx", pairs)

    gate_values = pl.pallas_call(
        lambda *refs: gate_kernel(inner_count, counts, *refs),
        in_specs=[SMEM] + any_of(blocks) + any_of(gate_pieces),
        out_specs=VMEM,
        out_shape=sds((total, width_mine), BF16),
        scratch_shapes=scratch(width_mine, 0, 0),
        compiler_params=limit,
        name="gate",
    )(place, *blocks, *gate_pieces)

    gated = pl.pallas_call(
        scan_kernel,
        in_specs=[SMEM] + [VMEM] * 8,
        out_specs=VMEM,
        out_shape=sds((total, width_mine), BF16),
        compiler_params=limit,
        name="scan",
    )(place, b_vals, c_vals, x_vals, gate_values, step, cum, states, prior)

    teams = [[t * members + m for m in range(members)] for t in range(ctx_count // TEAM)]
    parts = lax.all_to_all(
        gated, ("ctx", "inner"), 0, 0, axis_index_groups=teams, tiled=True
    ).reshape(members, row_count, width_mine)
    return pl.pallas_call(
        lambda *refs: norm_kernel(inner_count, *refs),
        in_specs=[VMEM, VMEM],
        out_specs=VMEM,
        out_shape=sds((row_count, H * P_SIZE), BF16),
        compiler_params=limit,
        name="norm",
    )(parts, norm_gain.reshape(1, -1))


def solution(mesh):
    placed = (
        P(("ctx", "inner"), None),
        P("ctx", None, "inner"),
        P("ctx", None, "inner"),
        P("ctx", "inner"),
        P(None, "inner"),
        P(),
        P("inner"),
        P("inner"),
        P(),
    )
    return jax.shard_map(
        on_device, mesh=mesh, in_specs=placed, out_specs=P(("ctx", "inner"), None), check_vma=False
    )
```

```python
import jax
import jax.numpy as jnp
from jax import lax
from jax.experimental import pallas as pl
from jax.experimental.pallas import tpu as pltpu
from jax.sharding import PartitionSpec as P


H = 64
P_SIZE = 64
N = 128
G = 4
CONV = 4
SPAN = 128
TEAM = 4
HALO = 16
LANES = 128
PAD = 8

EPSILON = 1e-05


ANY = pl.BlockSpec(memory_space=pl.ANY)
VMEM = pl.BlockSpec(memory_space=pltpu.VMEM)
SMEM = pl.BlockSpec(memory_space=pltpu.SMEM)
SMALL = pltpu.CompilerParams(vmem_limit_bytes=6 << 20)
F32 = jnp.float32
BF16 = jnp.bfloat16


def swapped(x, axis, mask):
    pairs = [(i, i ^ mask) for i in range(lax.axis_size(axis))]
    return lax.ppermute(x, axis, pairs)


def inner_blocks(block, place, inner_count, ctx_count):
    if inner_count != 4:
        got = [block]
        step = 1
        while step < inner_count:
            got = got + [swapped(b, "inner", step) for b in got]
            step *= 2
        return got
    near_x = swapped(block, "inner", 1)
    near_y = swapped(block, "inner", 2)
    pairs = []
    for c in range(ctx_count):
        for i in range(inner_count):
            pairs.append((c * inner_count + i, c * inner_count + (i ^ (1 if c % 2 else 2))))
    onward = pl.pallas_call(
        either_kernel,
        in_specs=[SMEM, ANY, ANY],
        out_specs=VMEM,
        out_shape=jax.ShapeDtypeStruct(block.shape, block.dtype),
        scratch_shapes=[pltpu.SemaphoreType.DMA],
        compiler_params=SMALL,
        name="either",
    )(place, near_x, near_y)
    far = lax.ppermute(onward, ("ctx", "inner"), pairs)
    return [block, near_x, near_y, far]


def gathered_rows(piece_of, z_count):
    return [piece_of(d) if d == 0 else swapped(piece_of(d), "ctx", 2 * d) for d in range(z_count)]


def fetch_weights(place, parts, scratch, sems):
    z_id, core = place[2], place[3]
    copies = []
    for index, (view, d, m) in enumerate(parts):
        rows = view.shape[0]
        row = pl.multiple_of((2 * (z_id ^ d) + (core ^ m)) * rows, rows)
        copies.append(pltpu.make_async_copy(view, scratch.at[pl.ds(row, rows)], sems.at[index]))
    for copy in copies:
        copy.start()
    return copies


def prepare_kernel(heads_mine, place, project, state, step, taps, mixer_taps, step_bias, decay_log, *outs):
    x_same, x_opposite, gate_same, gate_opposite, gate_sent, state_turned, step_same, step_opposite, taps_state = outs[:9]
    taps_mixer, bias, rate = outs[9:]
    side, core = place[4], place[3]
    pair = x_same.shape[1]
    width = pair // 2

    def columns(kind, index, size):
        if size % LANES == 0:
            return project[:, kind, pl.ds(pl.multiple_of(index * size, size), size)]
        got = project[:, kind, :size]
        for k in range(1, project.shape[2] // size):
            got = jnp.where(index == k, project[:, kind, k * size : (k + 1) * size], got)
        return got

    other_side = 1 - side
    x_same[...] = columns(1, side, pair)
    x_opposite[...] = columns(1, other_side, pair)
    gate_same[...] = columns(0, 2 * side + core, width)
    gate_opposite[...] = columns(0, 2 * other_side + core, width)
    gate_sent[:, :width] = columns(0, 2 * side + 1 - core, width)
    gate_sent[:, width:] = columns(0, 2 * other_side + 1 - core, width)
    cols = state.shape[2]
    target = lax.broadcasted_iota(jnp.int32, (2 * cols, cols), 0)
    source = lax.broadcasted_iota(jnp.int32, (2 * cols, cols), 1)
    per = cols // G
    turned = 0.0
    for part in range(2):
        wanted = (source % G) * 2 * per + part * per + source // G
        turned = turned + lax.dot_general(
            (target == wanted).astype(BF16),
            state[:, part, :],
            (((1,), (1,)), ((), ())),
            preferred_element_type=F32,
        )
    state_turned[...] = turned.astype(BF16)
    heads = step.shape[1]
    rows = step.shape[0]
    wide = jnp.concatenate([step[...].astype(F32), jnp.zeros((rows, LANES - heads), F32)], axis=1)
    turned_step = wide.T[: 2 * PAD]
    half = heads // 2
    low = turned_step[:PAD]
    high = turned_step[half : half + PAD]
    step_same[...] = jnp.where(side == 0, low, high).astype(BF16)
    step_opposite[...] = jnp.where(side == 0, high, low).astype(BF16)
    source = lax.broadcasted_iota(jnp.int32, (taps.shape[2], N), 0)
    target = lax.broadcasted_iota(jnp.int32, (taps.shape[2], N), 1)
    chosen = (source == target * G + place[5]).astype(F32)
    mine = jnp.where(core == 0, taps[:, 0, :], taps[:, 1, :])
    taps_state[: CONV + 1] = exact_dot(mine, chosen, ((1,), (0,)))
    quarter = place[0]
    if width % LANES == 0:
        taps_mixer[: CONV + 1] = mixer_taps[:, pl.ds(pl.multiple_of(quarter * width, width), width)]
    else:
        got = mixer_taps[:, :width]
        for k in range(1, TEAM):
            got = jnp.where(quarter == k, mixer_taps[:, k * width : (k + 1) * width], got)
        taps_mixer[: CONV + 1] = got
    row = lax.broadcasted_iota(jnp.int32, (PAD, heads), 0)
    column = lax.broadcasted_iota(jnp.int32, (PAD, heads), 1)
    own = jnp.logical_and(column == quarter * heads_mine + row, row < heads_mine)
    for values, out in ((step_bias[...], bias), (-jnp.exp(decay_log[...]), rate)):
        picked = jnp.sum(jnp.where(own, values, 0.0), axis=1, keepdims=True)
        out[...] = jnp.broadcast_to(picked, out.shape)


def either_kernel(place, first, second, out, sem):
    for core, values in enumerate((first, second)):

        @pl.when(place[3] == core)
        def _():
            copy = pltpu.make_async_copy(values, out, sem)
            copy.start()
            copy.wait()


def partner_columns_kernel(place, *refs):
    pieces, out = refs[:-1], refs[-1]
    width = out.shape[2]
    other = 1 - place[3]
    for d, piece in enumerate(pieces):
        if width % LANES == 0:
            out[d] = piece[:, pl.ds(pl.multiple_of(other * width, width), width)]
        else:
            out[d] = jnp.where(other == 0, piece[:, :width], piece[:, width:])


def partner_rows_kernel(place, *refs):
    pieces, out = refs[:-1], refs[-1]
    other = pl.multiple_of((1 - place[3]) * N, N)
    for d, piece in enumerate(pieces):
        out[d, :N] = piece[pl.ds(other, N), :]
        out[d, N:] = piece[2 * N :, :]


def payload_kernel(place, turned, *refs):
    received, steps, outs = refs[:-4], refs[-4:-2], refs[-2:]
    inner_id = place[1]
    rows = turned.shape[0] // G
    part = rows // 2
    for d in range(len(received) + 1):
        piece = received[d - 1] if d else turned.at[pl.ds(pl.multiple_of(place[5] * rows, rows), rows)]
        for k in range(2):
            start = pl.multiple_of(k * N + (inner_id ^ d) * part, part)
            for out in outs:
                out[pl.ds(start, part), :] = piece[k * part : (k + 1) * part, :]
    for step, out in zip(steps, outs):
        out[2 * N :, :] = step[...]


def sent_kernel(group_of, place, turned, *outs):
    rows = turned.shape[0] // G
    for d, out in enumerate(outs):
        start = pl.multiple_of(group_of(place[1] ^ (d + 1)) * rows, rows)
        out[...] = turned[pl.ds(start, rows), :]


def assemble_kernel(heads_mine, place, sent, *refs):
    pieces, out = refs[:-1], refs[-1]
    z_id, core = place[2], place[3]
    rows = pieces[0].shape[1]
    for d, piece in enumerate(pieces):
        own = piece[pl.ds(pl.multiple_of(core * N, N), N), :]
        for m, (state, step) in enumerate(((own, piece[2 * N :, :]), (sent[d, :N, :], sent[d, N:, :]))):
            step = step.astype(F32)
            mine = jnp.where(core == 0, step[:heads_mine], step[heads_mine : 2 * heads_mine])
            packed = jnp.concatenate(
                [state.astype(F32), mine, jnp.zeros((LANES - heads_mine, rows), F32)], axis=0
            )
            row = pl.multiple_of((2 * (z_id ^ d) + (core ^ m)) * rows, rows)
            out[pl.ds(row, rows), :] = packed.T.astype(BF16)


def tail_kernel(place, *refs):
    blocks, out, sem = refs[:-2], refs[-2], refs[-1]
    last = len(blocks) - 1
    for d, block in enumerate(blocks):

        @pl.when(place[1] == (last ^ d))
        def _():
            copy = pltpu.make_async_copy(block.at[pl.ds(block.shape[0] - HALO, HALO)], out, sem)
            copy.start()
            copy.wait()


def fetch_blocks(place, blocks, scratch, sems, inner_count, offset):
    inner_id = place[1]
    rows = blocks[0].shape[0]
    copies = []
    for d, block in enumerate(blocks):
        j, di = d // inner_count, d % inner_count
        row = pl.multiple_of(offset + j * inner_count * rows + (inner_id ^ di) * rows, HALO)
        copies.append(pltpu.make_async_copy(block, scratch.at[pl.ds(row, rows)], sems.at[d]))
    for copy in copies:
        copy.start()
    return copies


def wide_dot(a, b):
    return jnp.dot(a, b, preferred_element_type=F32)


def exact_dot(a, b, dims):
    return lax.dot_general(a, b, (dims, ((), ())), precision=lax.Precision.HIGHEST, preferred_element_type=F32)


def convolved(pre, taps, block):
    window = pre[pl.ds(pl.multiple_of(block * SPAN, SPAN), SPAN + HALO), :].astype(F32)
    start = HALO - (CONV - 1)
    mixed = taps[CONV : CONV + 1, :] + taps[0:1, :] * window[start : start + SPAN]
    for k in range(1, CONV):
        mixed = mixed + taps[k : k + 1, :] * window[start + k : start + k + SPAN]
    return mixed / (1.0 + jnp.exp(-mixed))


def spread(width):
    row = lax.broadcasted_iota(jnp.int32, (PAD, width), 0)
    column = lax.broadcasted_iota(jnp.int32, (PAD, width), 1)
    return (column // P_SIZE == row).astype(F32)


def projected(place, source, parts, tok, weight, sems, wsems, inner_count, keep):
    waits = fetch_weights(place, parts, weight, wsems) if parts else []
    blocks = source[:-1]
    span = (tok.shape[0] - HALO) // TEAM
    copies = []
    if blocks:
        top = pltpu.make_async_copy(source[-1], tok.at[pl.ds(0, HALO)], sems.at[len(blocks)])
        top.start()
        copies = fetch_blocks(place, blocks, tok, sems, inner_count, HALO)
        waits = waits + [top]
    for copy in waits:
        copy.wait()
    for j in range(TEAM):
        for di in range(inner_count if blocks else 0):
            copies[j * inner_count + di].wait()
        first = 0 if j == 0 else HALO + j * span
        size = span + (HALO if j == 0 else 0)
        keep(wide_dot(tok[pl.ds(first, size), :], weight[...]), j)


def state_kernel(inner_count, place, taps, bias, rate, weight, *refs):
    source, refs = refs[:-6], refs[-6:]
    half_out, step_out, cum_out, tok, pre, sems = refs
    span = (tok.shape[0] - HALO) // TEAM
    quarter = place[0]

    def keep(result, j):
        if j == 0:
            pre[pl.ds(0, HALO), :] = result[:HALO, :N].astype(BF16)
            result = result[HALO:]
        whose = quarter ^ j
        pre[pl.ds(pl.multiple_of(HALO + whose * span, HALO), span), :] = result[:, :N].astype(BF16)
        raw = result[:, N:].astype(BF16).astype(F32)
        for b in range(span // SPAN):
            turned = raw[b * SPAN : (b + 1) * SPAN].T
            step_out[whose * (span // SPAN) + b] = turned[:PAD]

    projected(place, source, (), tok, weight, sems, None, inner_count, keep)

    total = step_out.shape[0] * PAD
    raw = step_out[...] + bias[...][None]
    step = jnp.maximum(raw, 0.0) + jnp.log1p(jnp.exp(-jnp.abs(raw)))
    step_out[...] = step
    logdec = (step * rate[...][None]).reshape(total, SPAN)
    row = lax.broadcasted_iota(jnp.int32, (SPAN, SPAN), 0)
    column = lax.broadcasted_iota(jnp.int32, (SPAN, SPAN), 1)
    upper = (row <= column).astype(F32)
    cum_out[...] = exact_dot(logdec, upper, ((1,), (0,))).reshape(step_out.shape)

    def one(p, _):
        half_out[pl.ds(pl.multiple_of(p * SPAN, SPAN), SPAN), :] = convolved(pre, taps, p).astype(BF16)
        return 0

    lax.fori_loop(0, step_out.shape[0], one, 0, unroll=2)


def mixer_kernel(inner_count, shared, z_count, place, taps, half, half_other, step, cum, other, *refs):
    pieces, refs = refs[:z_count], refs[z_count:]
    tail = 8 if shared else 9
    source, refs = refs[:-tail], refs[-tail:]
    if shared:
        tok, source = source[0], ()
        x_out, states_out, last_out, through_out, weight, pre, sems, wsems = refs
        source = (None,)
    else:
        x_out, states_out, last_out, through_out, tok, weight, pre, sems, wsems = refs
    span = (tok.shape[0] - HALO) // TEAM
    quarter, core = place[0], place[3]
    width = x_out.shape[1]
    parts = []
    for d, piece in enumerate(pieces):
        view = piece
        if piece.shape[1] != width:
            view = piece.at[:, pl.ds(pl.multiple_of(core * width, width), width)]
        parts += [(view, d, 0), (other.at[d], d, 1)]

    def keep(result, j):
        if j == 0:
            pre[pl.ds(0, HALO), :] = result[:HALO].astype(BF16)
            result = result[HALO:]
        whose = quarter ^ j
        pre[pl.ds(pl.multiple_of(HALO + whose * span, HALO), span), :] = result.astype(BF16)

    projected(place, source, parts, tok, weight, sems, wsems, inner_count, keep)
    heads = spread(width)

    def one(p, carry):
        state, log_sum = carry
        rows = pl.ds(pl.multiple_of(p * SPAN, SPAN), SPAN)
        x = convolved(pre, taps, p).astype(BF16)
        x_out[rows, :] = x
        states_out[p] = state
        cum_p = cum[p]
        ends = cum_p[:, SPAN - 1 :]
        to_end = jnp.exp(ends - cum_p) * step[p]
        scaled = (x.astype(F32) * exact_dot(to_end, heads, ((0,), (0,)))).astype(BF16)
        b = jnp.where(core == 0, half[rows, :], half_other[rows, :])
        fresh = lax.dot_general(b, scaled, (((0,), (0,)), ((), ())), preferred_element_type=F32)
        end_row = jnp.sum(ends * heads, axis=0, keepdims=True)
        return jnp.exp(end_row) * state + fresh, log_sum + end_row

    state, log_sum = lax.fori_loop(
        0, step.shape[0], one, (jnp.zeros((N, width), F32), jnp.zeros((1, width), F32)), unroll=2
    )
    last_out[...] = state.astype(BF16)
    through_out[...] = jnp.broadcast_to(jnp.exp(log_sum), through_out.shape)


def gate_kernel(inner_count, shared, z_count, place, *refs):
    pieces, refs = refs[:z_count], refs[z_count:]
    tail = 4 if shared else 5
    source, refs = refs[:-tail], refs[-tail:]
    if shared:
        tok = source[0]
        source = (None,)
        gate_out, weight, sems, wsems = refs
    else:
        gate_out, tok, weight, sems, wsems = refs
    span = (tok.shape[0] - HALO) // TEAM
    quarter = place[0]
    parts = []
    for d, piece in enumerate(pieces):
        rows = piece.shape[0] // 2
        parts += [(piece.at[pl.ds(m * rows, rows)], d, m) for m in range(2)]

    def keep(result, j):
        result = result[HALO:] if j == 0 else result
        gate_out[pl.ds(pl.multiple_of((quarter ^ j) * span, span), span), :] = result.astype(BF16)

    projected(place, source, parts, tok, weight, sems, wsems, inner_count, keep)


def scan_kernel(place, half, half_other, x_vals, gate, step, cum, states, prior, gated_out):
    width = x_vals.shape[1]
    heads_mine = width // P_SIZE
    heads = spread(width)
    core = place[3]
    lane = lax.broadcasted_iota(jnp.int32, (SPAN, width), 1) // P_SIZE
    row = lax.broadcasted_iota(jnp.int32, (SPAN, SPAN), 0)
    column = lax.broadcasted_iota(jnp.int32, (SPAN, SPAN), 1)
    lower = column <= row
    entering = prior[...].astype(F32)

    def one(p, before):
        rows = pl.ds(pl.multiple_of(p * SPAN, SPAN), SPAN)
        first, second = half[rows, :], half_other[rows, :]
        b = jnp.where(core == 0, first, second)
        c = jnp.where(core == 0, second, first)
        x = x_vals[rows, :]
        cum_p = cum[p]
        step_p = step[p]
        scores = lax.dot_general(
            c, b, (((1,), (1,)), ((), ())), preferred_element_type=F32
        )
        cum_t = cum_p.T
        mixes = []
        parts = []
        for h in range(heads_mine):
            spacing = jnp.where(lower, cum_t[:, h : h + 1] - cum_p[h : h + 1, :], -jnp.inf)
            mixes.append((scores * jnp.exp(spacing) * step_p[h : h + 1, :]).astype(BF16))
            parts.append(jnp.where(lane == h, x, jnp.zeros_like(x)))
        diagonal = wide_dot(jnp.concatenate(mixes, axis=1), jnp.concatenate(parts, axis=0))
        state = states[p] + jnp.exp(before) * entering
        decay = exact_dot(jnp.exp(cum_p), heads, ((0,), (0,)))
        y = diagonal + decay * wide_dot(c, state.astype(BF16))
        g = gate[rows, :].astype(F32)
        gated_out[rows, :] = (y * (g / (1.0 + jnp.exp(-g)))).astype(BF16)
        return before + jnp.sum(cum_p[:, SPAN - 1 :] * heads, axis=0, keepdims=True)

    lax.fori_loop(0, step.shape[0], one, jnp.zeros((1, width), F32), unroll=2)


def norm_kernel(inner_count, parts, gain, out):
    width = parts.shape[2]
    group_width = H * P_SIZE // G
    for g in range(G):
        members = []
        power = 0.0
        for c in range(g * group_width, (g + 1) * group_width, width):
            index = c // width
            i, k = index // TEAM, index % TEAM
            wide = parts[k * inner_count + i].astype(F32)
            members.append((c, wide))
            power = power + jnp.sum(wide * wide, axis=1, keepdims=True)
        scale = lax.rsqrt(power / group_width + EPSILON)
        for c, wide in members:
            out[:, c : c + width] = (wide * scale * gain[:, c : c + width]).astype(BF16)


def on_device(
    tokens,
    project_weight,
    state_weight,
    step_weight,
    mixer_taps,
    state_taps,
    step_bias,
    decay_log,
    norm_gain,
):
    ctx_count = lax.axis_size("ctx")
    inner_count = lax.axis_size("inner")
    ctx_id = lax.axis_index("ctx")
    inner_id = lax.axis_index("inner")
    core = ctx_id % 2
    z_id = ctx_id // 2
    z_count = ctx_count // 2
    side = z_id % 2
    quarter = ctx_id % TEAM
    members = TEAM * inner_count

    rows_here, _, width_here = project_weight.shape
    row_count, model_width = tokens.shape
    heads_here = step_weight.shape[1]
    heads_mine = heads_here // TEAM
    width_mine = width_here // TEAM
    per_group = H // G
    group = inner_id * heads_here // per_group
    place = jnp.stack([quarter, inner_id, z_id, core, side, group]).astype(jnp.int32)
    total = members * row_count
    count = total // SPAN

    def sds(shape, dtype):
        return jax.ShapeDtypeStruct(shape, dtype)

    partner = swapped(tokens, "ctx", 2)
    near = inner_blocks(tokens, place, inner_count, ctx_count)
    beyond = inner_blocks(partner, place, inner_count, ctx_count)
    blocks = (
        near
        + [swapped(b, "ctx", 1) for b in near]
        + beyond
        + [swapped(b, "ctx", 1) for b in beyond]
    )
    tail = pl.pallas_call(
        tail_kernel,
        in_specs=[SMEM] + [ANY] * len(near),
        out_specs=VMEM,
        out_shape=sds((HALO, model_width), BF16),
        scratch_shapes=[pltpu.SemaphoreType.DMA],
        compiler_params=SMALL,
        name="tail",
    )(place, *near)
    halo = jnp.zeros_like(tail)
    for k in range(TEAM):
        pairs = [(c - 1, c + k) for c in range(TEAM, ctx_count, TEAM)]
        halo = halo + lax.ppermute(tail, "ctx", pairs)

    pair = 2 * width_mine
    slice_cols = state_weight.shape[2]
    prepared = pl.pallas_call(
        lambda *refs: prepare_kernel(heads_mine, *refs),
        in_specs=[SMEM] + [VMEM] * 7,
        out_specs=[VMEM] * 12,
        out_shape=[
            sds((rows_here, pair), BF16),
            sds((rows_here, pair), BF16),
            sds((rows_here, width_mine), BF16),
            sds((rows_here, width_mine), BF16),
            sds((rows_here, pair), BF16),
            sds((2 * slice_cols, rows_here), BF16),
            sds((PAD, rows_here), BF16),
            sds((PAD, rows_here), BF16),
            sds((PAD, N), F32),
            sds((PAD, width_mine), F32),
            sds((PAD, SPAN), F32),
            sds((PAD, SPAN), F32),
        ],
        compiler_params=SMALL,
        name="prepare",
    )(
        place,
        project_weight,
        state_weight,
        step_weight,
        state_taps,
        mixer_taps,
        step_bias.reshape(1, -1),
        decay_log.reshape(1, -1),
    )
    x_sides, gate_mine, gate_sent = prepared[0:2], prepared[2:4], prepared[4]
    state_turned, step_sides = prepared[5], prepared[6:8]

    x_pieces = gathered_rows(lambda d: x_sides[d % 2], z_count)

    def of_core(piece, which):
        return lax.dynamic_slice_in_dim(piece, which * width_mine, width_mine, 1)

    x_sent = pl.pallas_call(
        partner_columns_kernel,
        in_specs=[SMEM] + [VMEM] * z_count,
        out_specs=VMEM,
        out_shape=sds((z_count, rows_here, width_mine), BF16),
        compiler_params=SMALL,
        name="xsplit",
    )(place, *x_pieces)
    x_other = swapped(x_sent, "ctx", 1)
    if width_mine % LANES:
        x_pieces = [of_core(p, core) for p in x_pieces]

    part_rows = 2 * slice_cols // G
    if part_rows % (2 * HALO) == 0:
        sent = pl.pallas_call(
            lambda *refs: sent_kernel(lambda j: j * heads_here // per_group, *refs),
            in_specs=[SMEM, VMEM],
            out_specs=[VMEM] * (inner_count - 1),
            out_shape=[sds((part_rows, rows_here), BF16)] * (inner_count - 1),
            compiler_params=SMALL,
            name="sent",
        )(place, state_turned)
        received = [swapped(sent[d - 1], "inner", d) for d in range(1, inner_count)]
        payloads = pl.pallas_call(
            payload_kernel,
            in_specs=[SMEM] + [VMEM] * (inner_count + 2),
            out_specs=[VMEM] * 2,
            out_shape=[sds((2 * N + PAD, rows_here), BF16)] * 2,
            compiler_params=SMALL,
            name="payload",
        )(place, state_turned, *received, *step_sides)
    else:
        to_each = jnp.concatenate(
            [
                lax.slice_in_dim(state_turned, g * part_rows, (g + 1) * part_rows, axis=0)
                for g in [(j * heads_here) // per_group for j in range(inner_count)]
            ],
            axis=0,
        ).reshape(inner_count, part_rows, rows_here)
        state_rows = lax.all_to_all(to_each, "inner", 0, 0, tiled=True)
        state_rows = state_rows.reshape(inner_count, 2, part_rows // 2, rows_here)
        state_rows = state_rows.transpose(1, 0, 2, 3).reshape(2 * N, rows_here)
        payloads = [jnp.concatenate([state_rows, s], axis=0) for s in step_sides]
    state_pieces = gathered_rows(lambda d: payloads[d % 2], z_count)
    state_sent = pl.pallas_call(
        partner_rows_kernel,
        in_specs=[SMEM] + [VMEM] * z_count,
        out_specs=VMEM,
        out_shape=sds((z_count, N + PAD, rows_here), BF16),
        compiler_params=SMALL,
        name="ssplit",
    )(place, *state_pieces)
    state_other = swapped(state_sent, "ctx", 1)
    state_matrix = pl.pallas_call(
        lambda *refs: assemble_kernel(heads_mine, *refs),
        in_specs=[SMEM] + [VMEM] * (1 + z_count),
        out_specs=VMEM,
        out_shape=sds((model_width, N + LANES), BF16),
        compiler_params=SMALL,
        name="assemble",
    )(place, state_other, *state_pieces)

    gate_other = swapped(gate_sent, "ctx", 1)
    gate_chip = [
        jnp.concatenate([gate_mine[s], gate_other[:, s * width_mine : (s + 1) * width_mine]], axis=0)
        for s in range(2)
    ]
    gate_pieces = gathered_rows(lambda d: gate_chip[d % 2], z_count)

    taps_state, taps_mine, bias_mine, rate_mine = prepared[8:]

    shared = total * model_width <= 2**23
    tok_shape = (HALO + total, model_width)
    held = 2 * tok_shape[0] * model_width
    limit = pltpu.CompilerParams(vmem_limit_bytes=min(60 << 20, held + (4 << 20 if shared else 22 << 20)))

    def scratch(width, pre_width, own_tok):
        made = [pltpu.VMEM(tok_shape, BF16)] if own_tok else []
        if width:
            made.append(pltpu.VMEM((model_width, width), BF16))
        if pre_width:
            made.append(pltpu.VMEM((HALO + total, pre_width), BF16))
        return made + [pltpu.SemaphoreType.DMA((members + 1,)), pltpu.SemaphoreType.DMA((2 * z_count,))]

    source = list(blocks) + [halo]
    any_of = lambda values: [ANY] * len(values)
    state_outs = [sds((total, N), BF16), sds((count, PAD, SPAN), F32), sds((count, PAD, SPAN), F32)]
    outs = pl.pallas_call(
        lambda *refs: state_kernel(inner_count, *refs),
        in_specs=[SMEM, VMEM, VMEM, VMEM, VMEM] + any_of(source),
        out_specs=[VMEM] * (4 if shared else 3),
        out_shape=state_outs + ([sds(tok_shape, BF16)] if shared else []),
        scratch_shapes=scratch(0, N, not shared)[:-1],
        compiler_params=limit,
        name="state",
    )(place, taps_state, bias_mine, rate_mine, state_matrix, *source)
    half, step, cum = outs[:3]
    if shared:
        source = [outs[3]]
    held_spec = [VMEM] if shared else any_of(source)
    half_other = swapped(half, "ctx", 1)

    x_vals, states, last_state, through = pl.pallas_call(
        lambda *refs: mixer_kernel(inner_count, shared, z_count, *refs),
        in_specs=[SMEM, VMEM, VMEM, VMEM, VMEM, VMEM, ANY] + any_of(x_pieces) + held_spec,
        out_specs=[VMEM, VMEM, VMEM, VMEM],
        out_shape=[
            sds((total, width_mine), BF16),
            sds((count, N, width_mine), F32),
            sds((N, width_mine), BF16),
            sds((PAD, width_mine), F32),
        ],
        scratch_shapes=scratch(width_mine, width_mine, not shared),
        compiler_params=limit,
        name="mixer",
    )(place, taps_mine, half, half_other, step, cum, x_other, *x_pieces, *source)

    hops = ctx_count // TEAM - 1
    pairs = [(c, c + TEAM) for c in range(ctx_count - TEAM)]
    prior = jnp.zeros_like(last_state)
    for hop in range(hops):
        sent = last_state
        if hop:
            sent = (through[:1] * prior.astype(F32) + last_state.astype(F32)).astype(BF16)
        prior = lax.ppermute(sent, "ctx", pairs)

    gate_values = pl.pallas_call(
        lambda *refs: gate_kernel(inner_count, shared, z_count, *refs),
        in_specs=[SMEM] + any_of(gate_pieces) + held_spec,
        out_specs=VMEM,
        out_shape=sds((total, width_mine), BF16),
        scratch_shapes=scratch(width_mine, 0, not shared),
        compiler_params=limit,
        name="gate",
    )(place, *gate_pieces, *source)

    gated = pl.pallas_call(
        scan_kernel,
        in_specs=[SMEM] + [VMEM] * 8,
        out_specs=VMEM,
        out_shape=sds((total, width_mine), BF16),
        compiler_params=limit,
        name="scan",
    )(place, half, half_other, x_vals, gate_values, step, cum, states, prior)

    teams = [[t * members + m for m in range(members)] for t in range(ctx_count // TEAM)]
    parts = lax.all_to_all(
        gated, ("ctx", "inner"), 0, 0, axis_index_groups=teams, tiled=True
    ).reshape(members, row_count, width_mine)
    return pl.pallas_call(
        lambda *refs: norm_kernel(inner_count, *refs),
        in_specs=[VMEM, VMEM],
        out_specs=VMEM,
        out_shape=sds((row_count, H * P_SIZE), BF16),
        compiler_params=limit,
        name="norm",
    )(parts, norm_gain.reshape(1, -1))


def solution(mesh):
    placed = (
        P(("ctx", "inner"), None),
        P("ctx", None, "inner"),
        P("ctx", None, "inner"),
        P("ctx", "inner"),
        P(None, "inner"),
        P(),
        P("inner"),
        P("inner"),
        P(),
    )

    return jax.shard_map(
        on_device, mesh=mesh, in_specs=placed, out_specs=P(("ctx", "inner"), None), check_vma=False
    )
```

```python
import functools

import jax
import jax.numpy as jnp
from jax import lax
from jax.experimental import pallas as pl
from jax.experimental.pallas import tpu as pltpu
from jax.sharding import PartitionSpec as P


H = 64
P_SIZE = 64
N = 128
G = 4
CONV = 4
SPAN = 128
TEAM = 4
HALO = 16
LANES = 128
PAD = 8

EPSILON = 1e-05


ANY = pl.BlockSpec(memory_space=pl.ANY)
HBM = pl.BlockSpec(memory_space=pltpu.HBM)
VMEM = pl.BlockSpec(memory_space=pltpu.VMEM)
SMALL = pltpu.CompilerParams(vmem_limit_bytes=6 << 20)
F32 = jnp.float32
BF16 = jnp.bfloat16


def group_of(inner_id, heads_over, members_over):
    return inner_id * heads_over if heads_over else lax.div(inner_id, members_over)


def here(heads_over, members_over):
    ctx_id = lax.axis_index("ctx")
    inner_id = lax.axis_index("inner")
    z_id = lax.shift_right_logical(ctx_id, 1)
    return (
        ctx_id & (TEAM - 1),
        inner_id,
        z_id,
        ctx_id & 1,
        z_id & 1,
        group_of(inner_id, heads_over, members_over),
    )


def swapped(x, axis, mask):
    pairs = [(i, i ^ mask) for i in range(lax.axis_size(axis))]
    return lax.ppermute(x, axis, pairs)


def inner_blocks(block, at, inner_count, ctx_count):
    if inner_count != 4:
        got = [block]
        step = 1
        while step < inner_count:
            got = got + [swapped(b, "inner", step) for b in got]
            step *= 2
        return got
    near_x = swapped(block, "inner", 1)
    near_y = swapped(block, "inner", 2)
    pairs = []
    for c in range(ctx_count):
        for i in range(inner_count):
            pairs.append((c * inner_count + i, c * inner_count + (i ^ (1 if c % 2 else 2))))
    onward = pl.pallas_call(
        at(either_kernel),
        in_specs=[ANY, ANY],
        out_specs=VMEM,
        out_shape=jax.ShapeDtypeStruct(block.shape, block.dtype),
        scratch_shapes=[pltpu.SemaphoreType.DMA],
        compiler_params=SMALL,
        name="either",
    )(near_x, near_y)
    far = lax.ppermute(onward, ("ctx", "inner"), pairs)
    return [block, near_x, near_y, far]


def gathered_rows(piece_of, z_count):
    return [piece_of(d) if d == 0 else swapped(piece_of(d), "ctx", 2 * d) for d in range(z_count)]


def fetch_weights(place, parts, scratch, sems):
    z_id, core = place[2], place[3]
    copies = []
    for index, (view, d, m) in enumerate(parts):
        rows = view.shape[0]
        row = pl.multiple_of((2 * (z_id ^ d) + (core ^ m)) * rows, rows)
        copies.append(pltpu.make_async_copy(view, scratch.at[pl.ds(row, rows)], sems.at[index]))
    for copy in copies:
        copy.start()
    return copies


def side_columns(project, kind, index, size):
    if size % LANES == 0:
        return project[:, kind, pl.ds(pl.multiple_of(index * size, size), size)]
    got = project[:, kind, :size]
    for k in range(1, project.shape[2] // size):
        got = jnp.where(index == k, project[:, kind, k * size : (k + 1) * size], got)
    return got


def mixer_columns_kernel(place, project, same, opposite, held, sems):
    chunks = held.shape[0]
    rows = held.shape[1]
    pair = same.shape[1]
    copies = [
        pltpu.make_async_copy(project.at[pl.ds(c * rows, rows)], held.at[c], sems.at[c]) for c in range(chunks)
    ]
    for copy in copies:
        copy.start()
    for c, copy in enumerate(copies):
        copy.wait()
        same[c * rows : (c + 1) * rows] = side_columns(held.at[c], 1, place[4], pair)
        opposite[c * rows : (c + 1) * rows] = side_columns(held.at[c], 1, 1 - place[4], pair)


def prepare_kernel(heads_mine, place, *refs):
    inputs, outs, held, sems = refs[:7], refs[7:17], refs[17:24], refs[24]
    copies = [pltpu.make_async_copy(a, b, sems.at[i]) for i, (a, b) in enumerate(zip(inputs, held))]
    for copy in copies:
        copy.start()
    project, state, step, taps, mixer_taps, step_bias, decay_log = held
    for copy in copies[1:]:
        copy.wait()
    gate_same, gate_opposite, gate_sent, state_turned, step_same, step_opposite, taps_state = outs[:7]
    taps_mixer, bias, rate = outs[7:]
    side, core = place[4], place[3]
    width = gate_same.shape[1]

    cols = state.shape[2]
    target = lax.broadcasted_iota(jnp.int32, (2 * cols, cols), 0)
    source = lax.broadcasted_iota(jnp.int32, (2 * cols, cols), 1)
    per = cols // G
    turned = 0.0
    for part in range(2):
        wanted = (source % G) * 2 * per + part * per + source // G
        turned = turned + lax.dot_general(
            (target == wanted).astype(BF16),
            state[:, part, :],
            (((1,), (1,)), ((), ())),
            preferred_element_type=F32,
        )
    state_turned[...] = turned.astype(BF16)
    heads = step.shape[0]
    half = heads // 2
    turned_step = jnp.concatenate([step[...].astype(F32), jnp.zeros((PAD, step.shape[1]), F32)], axis=0)
    low = turned_step[:PAD]
    high = turned_step[half : half + PAD]
    step_same[...] = jnp.where(side == 0, low, high).astype(BF16)
    step_opposite[...] = jnp.where(side == 0, high, low).astype(BF16)
    source = lax.broadcasted_iota(jnp.int32, (taps.shape[2], N), 0)
    target = lax.broadcasted_iota(jnp.int32, (taps.shape[2], N), 1)
    chosen = (source == target * G + place[5]).astype(F32)
    mine = jnp.where(core == 0, taps[:, 0, :], taps[:, 1, :])
    taps_state[: CONV + 1] = exact_dot(mine, chosen, ((1,), (0,)))
    quarter = place[0]
    if width % LANES == 0:
        taps_mixer[: CONV + 1] = mixer_taps[:, pl.ds(pl.multiple_of(quarter * width, width), width)]
    else:
        got = mixer_taps[:, :width]
        for k in range(1, TEAM):
            got = jnp.where(quarter == k, mixer_taps[:, k * width : (k + 1) * width], got)
        taps_mixer[: CONV + 1] = got
    row = lax.broadcasted_iota(jnp.int32, (PAD, heads), 0)
    column = lax.broadcasted_iota(jnp.int32, (PAD, heads), 1)
    own = jnp.logical_and(column == quarter * heads_mine + row, row < heads_mine)
    for values, out in ((step_bias[...], bias), (-jnp.exp(decay_log[...]), rate)):
        picked = jnp.sum(jnp.where(own, values, 0.0), axis=1, keepdims=True)
        out[...] = jnp.broadcast_to(picked, out.shape)
    copies[0].wait()
    other_side = 1 - side
    gate_same[...] = side_columns(project, 0, 2 * side + core, width)
    gate_opposite[...] = side_columns(project, 0, 2 * other_side + core, width)
    gate_sent[:, :width] = side_columns(project, 0, 2 * side + 1 - core, width)
    gate_sent[:, width:] = side_columns(project, 0, 2 * other_side + 1 - core, width)


def either_kernel(place, first, second, out, sem):
    for core, values in enumerate((first, second)):

        @pl.when(place[3] == core)
        def _():
            copy = pltpu.make_async_copy(values, out, sem)
            copy.start()
            copy.wait()


def partner_columns_kernel(place, *refs):
    pieces, out = refs[:-1], refs[-1]
    width = out.shape[2]
    other = 1 - place[3]
    for d, piece in enumerate(pieces):
        if width % LANES == 0:
            out[d] = piece[:, pl.ds(pl.multiple_of(other * width, width), width)]
        else:
            out[d] = jnp.where(other == 0, piece[:, :width], piece[:, width:])


def partner_rows_kernel(place, *refs):
    pieces, out = refs[:-1], refs[-1]
    other = pl.multiple_of((1 - place[3]) * N, N)
    for d, piece in enumerate(pieces):
        out[d, :N] = piece[pl.ds(other, N), :]
        out[d, N:] = piece[2 * N :, :]


def payload_kernel(place, turned, *refs):
    received, steps, outs = refs[:-4], refs[-4:-2], refs[-2:]
    inner_id = place[1]
    rows = turned.shape[0] // G
    part = rows // 2
    for d in range(len(received) + 1):
        piece = received[d - 1] if d else turned.at[pl.ds(pl.multiple_of(place[5] * rows, rows), rows)]
        for k in range(2):
            start = pl.multiple_of(k * N + (inner_id ^ d) * part, part)
            for out in outs:
                out[pl.ds(start, part), :] = piece[k * part : (k + 1) * part, :]
    for step, out in zip(steps, outs):
        out[2 * N :, :] = step[...]


def sent_kernel(group_of, place, turned, *outs):
    rows = turned.shape[0] // G
    for d, out in enumerate(outs):
        start = pl.multiple_of(group_of(place[1] ^ (d + 1)) * rows, rows)
        out[...] = turned[pl.ds(start, rows), :]


def assemble_kernel(heads_mine, place, sent, *refs):
    pieces, out = refs[:-1], refs[-1]
    z_id, core = place[2], place[3]
    rows = pieces[0].shape[1]
    for d, piece in enumerate(pieces):
        own = piece[pl.ds(pl.multiple_of(core * N, N), N), :]
        for m, (state, step) in enumerate(((own, piece[2 * N :, :]), (sent[d, :N, :], sent[d, N:, :]))):
            step = step.astype(F32)
            mine = jnp.where(core == 0, step[:heads_mine], step[heads_mine : 2 * heads_mine])
            packed = jnp.concatenate(
                [state.astype(F32), mine, jnp.zeros((LANES - heads_mine, rows), F32)], axis=0
            )
            row = pl.multiple_of((2 * (z_id ^ d) + (core ^ m)) * rows, rows)
            out[pl.ds(row, rows), :] = packed.T.astype(BF16)


def tail_kernel(place, *refs):
    blocks, out, sem = refs[:-2], refs[-2], refs[-1]
    inner_count = len(blocks) // 2
    for d, block in enumerate(blocks):
        away, di = d // inner_count, d % inner_count

        @pl.when(jnp.logical_and(place[3] == 1 - away, place[1] == (inner_count - 1) ^ di))
        def _():
            copy = pltpu.make_async_copy(block.at[pl.ds(block.shape[0] - HALO, HALO)], out, sem)
            copy.start()
            copy.wait()


def fetch_blocks(place, blocks, scratch, sems, inner_count, offset):
    inner_id = place[1]
    rows = blocks[0].shape[0]
    copies = []
    for d, block in enumerate(blocks):
        j, di = d // inner_count, d % inner_count
        row = pl.multiple_of(offset + j * inner_count * rows + (inner_id ^ di) * rows, HALO)
        copies.append(pltpu.make_async_copy(block, scratch.at[pl.ds(row, rows)], sems.at[d]))
    for copy in copies:
        copy.start()
    return copies


def wide_dot(a, b):
    return jnp.dot(a, b, preferred_element_type=F32)


def exact_dot(a, b, dims):
    return lax.dot_general(a, b, (dims, ((), ())), precision=lax.Precision.HIGHEST, preferred_element_type=F32)


def convolved(pre, taps, block):
    window = pre[pl.ds(pl.multiple_of(block * SPAN, SPAN), SPAN + HALO), :].astype(F32)
    start = HALO - (CONV - 1)
    mixed = taps[CONV : CONV + 1, :] + taps[0:1, :] * window[start : start + SPAN]
    for k in range(1, CONV):
        mixed = mixed + taps[k : k + 1, :] * window[start + k : start + k + SPAN]
    return mixed / (1.0 + jnp.exp(-mixed))


def spread(width):
    row = lax.broadcasted_iota(jnp.int32, (PAD, width), 0)
    column = lax.broadcasted_iota(jnp.int32, (PAD, width), 1)
    return (column // P_SIZE == row).astype(F32)


def projected(place, source, parts, tok, weight, sems, wsems, inner_count, keep):
    waits = fetch_weights(place, parts, weight, wsems) if parts else []
    blocks = source[:-1]
    span = (tok.shape[0] - HALO) // TEAM
    copies = []
    if blocks:
        top = pltpu.make_async_copy(source[-1], tok.at[pl.ds(0, HALO)], sems.at[len(blocks)])
        top.start()
        copies = fetch_blocks(place, blocks, tok, sems, inner_count, HALO)
        waits = waits + [top]
    for copy in waits:
        copy.wait()
    for j in range(TEAM):
        for di in range(inner_count if blocks else 0):
            copies[j * inner_count + di].wait()
        first = 0 if j == 0 else HALO + j * span
        size = span + (HALO if j == 0 else 0)
        keep(wide_dot(tok[pl.ds(first, size), :], weight[...]), j)


def state_kernel(inner_count, place, taps, bias, rate, weight, *refs):
    source, refs = refs[:-6], refs[-6:]
    half_out, step_out, cum_out, tok, pre, sems = refs
    span = (tok.shape[0] - HALO) // TEAM
    quarter = place[0]

    def keep(result, j):
        if j == 0:
            pre[pl.ds(0, HALO), :] = result[:HALO, :N].astype(BF16)
            result = result[HALO:]
        whose = quarter ^ j
        pre[pl.ds(pl.multiple_of(HALO + whose * span, HALO), span), :] = result[:, :N].astype(BF16)
        raw = result[:, N:].astype(BF16).astype(F32)
        for b in range(span // SPAN):
            turned = raw[b * SPAN : (b + 1) * SPAN].T
            step_out[whose * (span // SPAN) + b] = turned[:PAD]

    projected(place, source, (), tok, weight, sems, None, inner_count, keep)

    total = step_out.shape[0] * PAD
    raw = step_out[...] + bias[...][None]
    step = jnp.maximum(raw, 0.0) + jnp.log1p(jnp.exp(-jnp.abs(raw)))
    step_out[...] = step
    logdec = (step * rate[...][None]).reshape(total, SPAN)
    row = lax.broadcasted_iota(jnp.int32, (SPAN, SPAN), 0)
    column = lax.broadcasted_iota(jnp.int32, (SPAN, SPAN), 1)
    upper = (row <= column).astype(F32)
    cum_out[...] = exact_dot(logdec, upper, ((1,), (0,))).reshape(step_out.shape)

    def one(p, _):
        half_out[pl.ds(pl.multiple_of(p * SPAN, SPAN), SPAN), :] = convolved(pre, taps, p).astype(BF16)
        return 0

    lax.fori_loop(0, step_out.shape[0], one, 0, unroll=2)


def mixer_kernel(inner_count, shared, z_count, place, taps, half, half_other, step, cum, other, *refs):
    pieces, refs = refs[:z_count], refs[z_count:]
    tail = 8 if shared else 9
    source, refs = refs[:-tail], refs[-tail:]
    if shared:
        tok, source = source[0], ()
        x_out, states_out, last_out, through_out, weight, pre, sems, wsems = refs
        source = (None,)
    else:
        x_out, states_out, last_out, through_out, tok, weight, pre, sems, wsems = refs
    span = (tok.shape[0] - HALO) // TEAM
    quarter, core = place[0], place[3]
    width = x_out.shape[1]
    parts = []
    for d, piece in enumerate(pieces):
        view = piece
        if piece.shape[1] != width:
            view = piece.at[:, pl.ds(pl.multiple_of(core * width, width), width)]
        parts += [(view, d, 0), (other.at[d], d, 1)]

    def keep(result, j):
        if j == 0:
            pre[pl.ds(0, HALO), :] = result[:HALO].astype(BF16)
            result = result[HALO:]
        whose = quarter ^ j
        pre[pl.ds(pl.multiple_of(HALO + whose * span, HALO), span), :] = result.astype(BF16)

    projected(place, source, parts, tok, weight, sems, wsems, inner_count, keep)
    heads = spread(width)

    def one(p, carry):
        state, log_sum = carry
        rows = pl.ds(pl.multiple_of(p * SPAN, SPAN), SPAN)
        x = convolved(pre, taps, p).astype(BF16)
        x_out[rows, :] = x
        states_out[p] = state
        cum_p = cum[p]
        ends = cum_p[:, SPAN - 1 :]
        to_end = jnp.exp(ends - cum_p) * step[p]
        scaled = (x.astype(F32) * exact_dot(to_end, heads, ((0,), (0,)))).astype(BF16)
        b = jnp.where(core == 0, half[rows, :], half_other[rows, :])
        fresh = lax.dot_general(b, scaled, (((0,), (0,)), ((), ())), preferred_element_type=F32)
        end_row = jnp.sum(ends * heads, axis=0, keepdims=True)
        return jnp.exp(end_row) * state + fresh, log_sum + end_row

    state, log_sum = lax.fori_loop(
        0, step.shape[0], one, (jnp.zeros((N, width), F32), jnp.zeros((1, width), F32)), unroll=2
    )
    last_out[...] = state.astype(BF16)
    through_out[...] = jnp.broadcast_to(jnp.exp(log_sum), through_out.shape)


def gate_kernel(inner_count, shared, z_count, place, *refs):
    pieces, refs = refs[:z_count], refs[z_count:]
    tail = 4 if shared else 5
    source, refs = refs[:-tail], refs[-tail:]
    if shared:
        tok = source[0]
        source = (None,)
        gate_out, weight, sems, wsems = refs
    else:
        gate_out, tok, weight, sems, wsems = refs
    span = (tok.shape[0] - HALO) // TEAM
    quarter = place[0]
    parts = []
    for d, piece in enumerate(pieces):
        rows = piece.shape[0] // 2
        parts += [(piece.at[pl.ds(m * rows, rows)], d, m) for m in range(2)]

    def keep(result, j):
        result = result[HALO:] if j == 0 else result
        gate_out[pl.ds(pl.multiple_of((quarter ^ j) * span, span), span), :] = result.astype(BF16)

    projected(place, source, parts, tok, weight, sems, wsems, inner_count, keep)


def scan_kernel(place, half, half_other, x_vals, gate, step, cum, states, prior, gated_out):
    width = x_vals.shape[1]
    heads_mine = width // P_SIZE
    heads = spread(width)
    core = place[3]
    lane = lax.broadcasted_iota(jnp.int32, (SPAN, width), 1) // P_SIZE
    row = lax.broadcasted_iota(jnp.int32, (SPAN, SPAN), 0)
    column = lax.broadcasted_iota(jnp.int32, (SPAN, SPAN), 1)
    lower = column <= row
    entering = prior[...].astype(F32)

    def one(p, before):
        rows = pl.ds(pl.multiple_of(p * SPAN, SPAN), SPAN)
        first, second = half[rows, :], half_other[rows, :]
        b = jnp.where(core == 0, first, second)
        c = jnp.where(core == 0, second, first)
        x = x_vals[rows, :]
        cum_p = cum[p]
        step_p = step[p]
        scores = lax.dot_general(
            c, b, (((1,), (1,)), ((), ())), preferred_element_type=F32
        )
        cum_t = cum_p.T
        mixes = []
        parts = []
        for h in range(heads_mine):
            spacing = jnp.where(lower, cum_t[:, h : h + 1] - cum_p[h : h + 1, :], -jnp.inf)
            mixes.append((scores * jnp.exp(spacing) * step_p[h : h + 1, :]).astype(BF16))
            parts.append(jnp.where(lane == h, x, jnp.zeros_like(x)))
        diagonal = wide_dot(jnp.concatenate(mixes, axis=1), jnp.concatenate(parts, axis=0))
        state = states[p] + jnp.exp(before) * entering
        decay = exact_dot(jnp.exp(cum_p), heads, ((0,), (0,)))
        y = diagonal + decay * wide_dot(c, state.astype(BF16))
        g = gate[rows, :].astype(F32)
        gated_out[rows, :] = (y * (g / (1.0 + jnp.exp(-g)))).astype(BF16)
        return before + jnp.sum(cum_p[:, SPAN - 1 :] * heads, axis=0, keepdims=True)

    lax.fori_loop(0, step.shape[0], one, jnp.zeros((1, width), F32), unroll=2)


def norm_kernel(inner_count, parts, gain, out):
    width = parts.shape[2]
    group_width = H * P_SIZE // G
    for g in range(G):
        members = []
        power = 0.0
        for c in range(g * group_width, (g + 1) * group_width, width):
            index = c // width
            i, k = index // TEAM, index % TEAM
            wide = parts[k * inner_count + i].astype(F32)
            members.append((c, wide))
            power = power + jnp.sum(wide * wide, axis=1, keepdims=True)
        scale = lax.rsqrt(power / group_width + EPSILON)
        for c, wide in members:
            out[:, c : c + width] = (wide * scale * gain[:, c : c + width]).astype(BF16)


def on_device(
    tokens,
    project_weight,
    state_weight,
    step_weight,
    mixer_taps,
    state_taps,
    step_bias,
    decay_log,
    norm_gain,
):
    ctx_count = lax.axis_size("ctx")
    inner_count = lax.axis_size("inner")
    z_count = ctx_count // 2
    members = TEAM * inner_count

    rows_here, _, width_here = project_weight.shape
    row_count, model_width = tokens.shape
    heads_here = step_weight.shape[1]
    heads_mine = heads_here // TEAM
    width_mine = width_here // TEAM
    per_group = H // G
    spread_out = heads_here // per_group, per_group // heads_here

    def at(kernel):
        return lambda *refs: kernel(here(*spread_out), *refs)

    total = members * row_count
    count = total // SPAN

    def sds(shape, dtype):
        return jax.ShapeDtypeStruct(shape, dtype)

    partner = swapped(tokens, "ctx", 2)
    near = inner_blocks(tokens, at, inner_count, ctx_count)
    beyond = inner_blocks(partner, at, inner_count, ctx_count)
    blocks = near + [swapped(b, "ctx", 1) for b in near] + beyond + [swapped(b, "ctx", 1) for b in beyond]
    tail = pl.pallas_call(
        at(tail_kernel),
        in_specs=[ANY] * (2 * inner_count),
        out_specs=VMEM,
        out_shape=sds((HALO, model_width), BF16),
        scratch_shapes=[pltpu.SemaphoreType.DMA],
        compiler_params=SMALL,
        name="tail",
    )(*blocks[: 2 * inner_count])
    halo = jnp.zeros_like(tail)
    for k in range(2):
        pairs = [
            (c - 2 + m, c + 2 * k + m) for c in range(TEAM, ctx_count, TEAM) for m in range(2)
        ]
        halo = halo + lax.ppermute(tail, "ctx", pairs)

    pair = 2 * width_mine
    slice_cols = state_weight.shape[2]
    chunks = 4
    x_sides = pl.pallas_call(
        at(mixer_columns_kernel),
        in_specs=[HBM],
        out_specs=[VMEM] * 2,
        out_shape=[sds((rows_here, pair), BF16)] * 2,
        scratch_shapes=[
            pltpu.VMEM((chunks, rows_here // chunks, 2, width_here), BF16),
            pltpu.SemaphoreType.DMA((chunks,)),
        ],
        compiler_params=SMALL,
        name="columns",
    )(project_weight)
    to_prepare = (
        project_weight,
        state_weight,
        step_weight.T,
        state_taps,
        mixer_taps,
        step_bias.reshape(1, -1),
        decay_log.reshape(1, -1),
    )
    prepared = pl.pallas_call(
        at(functools.partial(prepare_kernel, heads_mine)),
        in_specs=[HBM] * 7,
        out_specs=[VMEM] * 10,
        out_shape=[
            sds((rows_here, width_mine), BF16),
            sds((rows_here, width_mine), BF16),
            sds((rows_here, pair), BF16),
            sds((2 * slice_cols, rows_here), BF16),
            sds((PAD, rows_here), BF16),
            sds((PAD, rows_here), BF16),
            sds((PAD, N), F32),
            sds((PAD, width_mine), F32),
            sds((PAD, SPAN), F32),
            sds((PAD, SPAN), F32),
        ],
        scratch_shapes=[pltpu.VMEM(v.shape, v.dtype) for v in to_prepare] + [pltpu.SemaphoreType.DMA((7,))],
        compiler_params=SMALL,
        name="prepare",
    )(*to_prepare)
    gate_mine, gate_sent = prepared[0:2], prepared[2]
    state_turned, step_sides = prepared[3], prepared[4:6]

    x_pieces = gathered_rows(lambda d: x_sides[d % 2], z_count)

    def of_core(piece, which):
        return lax.dynamic_slice_in_dim(piece, which * width_mine, width_mine, 1)

    x_sent = pl.pallas_call(
        at(partner_columns_kernel),
        in_specs=[VMEM] * z_count,
        out_specs=VMEM,
        out_shape=sds((z_count, rows_here, width_mine), BF16),
        compiler_params=SMALL,
        name="xsplit",
    )(*x_pieces)
    x_other = swapped(x_sent, "ctx", 1)
    if width_mine % LANES:
        x_pieces = [of_core(p, lax.axis_index("ctx") % 2) for p in x_pieces]

    part_rows = 2 * slice_cols // G
    if part_rows % (2 * HALO) == 0:
        sent = pl.pallas_call(
            at(functools.partial(sent_kernel, lambda j: group_of(j, *spread_out))),
            in_specs=[VMEM],
            out_specs=[VMEM] * (inner_count - 1),
            out_shape=[sds((part_rows, rows_here), BF16)] * (inner_count - 1),
            compiler_params=SMALL,
            name="sent",
        )(state_turned)
        received = [swapped(sent[d - 1], "inner", d) for d in range(1, inner_count)]
        payload_call = pl.pallas_call(
            at(payload_kernel),
            in_specs=[VMEM] * (inner_count + 2),
            out_specs=[VMEM] * 2,
            out_shape=[sds((2 * N + PAD, rows_here), BF16)] * 2,
            compiler_params=SMALL,
            name="payload",
        )
        payloads = payload_call(state_turned, *received, *step_sides)
    else:
        to_each = jnp.concatenate(
            [
                lax.slice_in_dim(state_turned, g * part_rows, (g + 1) * part_rows, axis=0)
                for g in [(j * heads_here) // per_group for j in range(inner_count)]
            ],
            axis=0,
        ).reshape(inner_count, part_rows, rows_here)
        state_rows = lax.all_to_all(to_each, "inner", 0, 0, tiled=True)
        state_rows = state_rows.reshape(inner_count, 2, part_rows // 2, rows_here)
        state_rows = state_rows.transpose(1, 0, 2, 3).reshape(2 * N, rows_here)
        payloads = [jnp.concatenate([state_rows, s], axis=0) for s in step_sides]
    state_pieces = gathered_rows(lambda d: payloads[d % 2], z_count)
    state_sent = pl.pallas_call(
        at(partner_rows_kernel),
        in_specs=[VMEM] * z_count,
        out_specs=VMEM,
        out_shape=sds((z_count, N + PAD, rows_here), BF16),
        compiler_params=SMALL,
        name="ssplit",
    )(*state_pieces)
    state_other = swapped(state_sent, "ctx", 1)
    state_matrix = pl.pallas_call(
        at(functools.partial(assemble_kernel, heads_mine)),
        in_specs=[VMEM] * (1 + z_count),
        out_specs=VMEM,
        out_shape=sds((model_width, N + LANES), BF16),
        compiler_params=SMALL,
        name="assemble",
    )(state_other, *state_pieces)

    gate_other = swapped(gate_sent, "ctx", 1)
    gate_chip = [
        jnp.concatenate([gate_mine[s], gate_other[:, s * width_mine : (s + 1) * width_mine]], axis=0)
        for s in range(2)
    ]
    gate_pieces = gathered_rows(lambda d: gate_chip[d % 2], z_count)

    taps_state, taps_mine, bias_mine, rate_mine = prepared[6:]

    shared = total * model_width <= 2**23
    tok_shape = (HALO + total, model_width)
    held = 2 * tok_shape[0] * model_width
    limit = pltpu.CompilerParams(vmem_limit_bytes=min(60 << 20, held + (4 << 20 if shared else 22 << 20)))

    def scratch(width, pre_width, own_tok):
        made = [pltpu.VMEM(tok_shape, BF16)] if own_tok else []
        if width:
            made.append(pltpu.VMEM((model_width, width), BF16))
        if pre_width:
            made.append(pltpu.VMEM((HALO + total, pre_width), BF16))
        return made + [pltpu.SemaphoreType.DMA((members + 1,)), pltpu.SemaphoreType.DMA((2 * z_count,))]

    source = list(blocks) + [halo]
    any_of = lambda values: [ANY] * len(values)
    state_outs = [sds((total, N), BF16), sds((count, PAD, SPAN), F32), sds((count, PAD, SPAN), F32)]
    outs = pl.pallas_call(
        at(functools.partial(state_kernel, inner_count)),
        in_specs=[VMEM] * 4 + any_of(source),
        out_specs=[VMEM] * (4 if shared else 3),
        out_shape=state_outs + ([sds(tok_shape, BF16)] if shared else []),
        scratch_shapes=scratch(0, N, not shared)[:-1],
        compiler_params=limit,
        name="state",
    )(taps_state, bias_mine, rate_mine, state_matrix, *source)
    half, step, cum = outs[:3]
    if shared:
        source = [outs[3]]
    held_spec = [VMEM] if shared else any_of(source)
    half_other = swapped(half, "ctx", 1)

    x_vals, states, last_state, through = pl.pallas_call(
        at(functools.partial(mixer_kernel, inner_count, shared, z_count)),
        in_specs=[VMEM] * 5 + [ANY] + any_of(x_pieces) + held_spec,
        out_specs=[VMEM, VMEM, VMEM, VMEM],
        out_shape=[
            sds((total, width_mine), BF16),
            sds((count, N, width_mine), F32),
            sds((N, width_mine), BF16),
            sds((PAD, width_mine), F32),
        ],
        scratch_shapes=scratch(width_mine, width_mine, not shared),
        compiler_params=limit,
        name="mixer",
    )(taps_mine, half, half_other, step, cum, x_other, *x_pieces, *source)

    hops = ctx_count // TEAM - 1
    pairs = [(c, c + TEAM) for c in range(ctx_count - TEAM)]
    prior = jnp.zeros_like(last_state)
    for hop in range(hops):
        sent = last_state
        if hop:
            sent = (through[:1] * prior.astype(F32) + last_state.astype(F32)).astype(BF16)
        prior = lax.ppermute(sent, "ctx", pairs)

    gate_values = pl.pallas_call(
        at(functools.partial(gate_kernel, inner_count, shared, z_count)),
        in_specs=any_of(gate_pieces) + held_spec,
        out_specs=VMEM,
        out_shape=sds((total, width_mine), BF16),
        scratch_shapes=scratch(width_mine, 0, not shared),
        compiler_params=limit,
        name="gate",
    )(*gate_pieces, *source)

    gated = pl.pallas_call(
        at(scan_kernel),
        in_specs=[VMEM] * 8,
        out_specs=VMEM,
        out_shape=sds((total, width_mine), BF16),
        compiler_params=limit,
        name="scan",
    )(half, half_other, x_vals, gate_values, step, cum, states, prior)

    teams = [[t * members + m for m in range(members)] for t in range(ctx_count // TEAM)]
    parts = lax.all_to_all(
        gated, ("ctx", "inner"), 0, 0, axis_index_groups=teams, tiled=True
    ).reshape(members, row_count, width_mine)
    return pl.pallas_call(
        lambda *refs: norm_kernel(inner_count, *refs),
        in_specs=[VMEM, VMEM],
        out_specs=VMEM,
        out_shape=sds((row_count, H * P_SIZE), BF16),
        compiler_params=limit,
        name="norm",
    )(parts, norm_gain.reshape(1, -1))


def solution(mesh):
    placed = (
        P(("ctx", "inner"), None),
        P("ctx", None, "inner"),
        P("ctx", None, "inner"),
        P("ctx", "inner"),
        P(None, "inner"),
        P(),
        P("inner"),
        P("inner"),
        P(),
    )

    return jax.shard_map(on_device, mesh=mesh, in_specs=placed, out_specs=P(("ctx", "inner"), None), check_vma=False)
```

```python
import functools

import jax
import jax.numpy as jnp
from jax import lax
from jax.experimental import pallas as pl
from jax.experimental.pallas import tpu as pltpu
from jax.sharding import PartitionSpec as P


H = 64
P_SIZE = 64
N = 128
G = 4
CONV = 4
SPAN = 128
TEAM = 4
HALO = 16
LANES = 128
PAD = 8

EPSILON = 1e-05


ANY = pl.BlockSpec(memory_space=pl.ANY)
HBM = pl.BlockSpec(memory_space=pltpu.HBM)
VMEM = pl.BlockSpec(memory_space=pltpu.VMEM)
SMALL = pltpu.CompilerParams(vmem_limit_bytes=6 << 20)
F32 = jnp.float32
BF16 = jnp.bfloat16


def group_of(inner_id, heads_over, members_over):
    return inner_id * heads_over if heads_over else lax.div(inner_id, members_over)


def here(heads_over, members_over):
    ctx_id = lax.axis_index("ctx")
    inner_id = lax.axis_index("inner")
    z_id = lax.shift_right_logical(ctx_id, 1)
    return (
        ctx_id & (TEAM - 1),
        inner_id,
        z_id,
        ctx_id & 1,
        z_id & 1,
        group_of(inner_id, heads_over, members_over),
    )


def swapped(x, axis, mask):
    pairs = [(i, i ^ mask) for i in range(lax.axis_size(axis))]
    return lax.ppermute(x, axis, pairs)


def inner_blocks(block, at, inner_count, ctx_count):
    if inner_count != 4:
        got = [block]
        step = 1
        while step < inner_count:
            got = got + [swapped(b, "inner", step) for b in got]
            step *= 2
        return got
    near_x = swapped(block, "inner", 1)
    near_y = swapped(block, "inner", 2)
    pairs = []
    for c in range(ctx_count):
        for i in range(inner_count):
            pairs.append((c * inner_count + i, c * inner_count + (i ^ (1 if c % 2 else 2))))
    onward = pl.pallas_call(
        at(either_kernel),
        in_specs=[ANY, ANY],
        out_specs=VMEM,
        out_shape=jax.ShapeDtypeStruct(block.shape, block.dtype),
        scratch_shapes=[pltpu.SemaphoreType.DMA],
        compiler_params=SMALL,
        name="either",
    )(near_x, near_y)
    far = lax.ppermute(onward, ("ctx", "inner"), pairs)
    return [block, near_x, near_y, far]


def gathered_rows(piece_of, z_count):
    return [piece_of(d) if d == 0 else swapped(piece_of(d), "ctx", 2 * d) for d in range(z_count)]


def fetch_weights(place, parts, scratch, sems):
    z_id, core = place[2], place[3]
    copies = []
    for index, (view, d, m) in enumerate(parts):
        rows = view.shape[0]
        row = pl.multiple_of((2 * (z_id ^ d) + (core ^ m)) * rows, rows)
        copies.append(pltpu.make_async_copy(view, scratch.at[pl.ds(row, rows)], sems.at[index]))
    for copy in copies:
        copy.start()
    return copies


def side_columns(project, kind, index, size):
    if size % LANES == 0:
        return project[:, kind, pl.ds(pl.multiple_of(index * size, size), size)]
    got = project[:, kind, :size]
    for k in range(1, project.shape[2] // size):
        got = jnp.where(index == k, project[:, kind, k * size : (k + 1) * size], got)
    return got


def mixer_columns_kernel(place, project, same, opposite, held, sems):
    chunks = held.shape[0]
    rows = held.shape[1]
    pair = same.shape[1]
    copies = [
        pltpu.make_async_copy(project.at[pl.ds(c * rows, rows)], held.at[c], sems.at[c]) for c in range(chunks)
    ]
    for copy in copies:
        copy.start()
    for c, copy in enumerate(copies):
        copy.wait()
        same[c * rows : (c + 1) * rows] = side_columns(held.at[c], 1, place[4], pair)
        opposite[c * rows : (c + 1) * rows] = side_columns(held.at[c], 1, 1 - place[4], pair)


def prepare_kernel(place, *refs):
    inputs, outs, held, sems = refs[:2], refs[2:5], refs[5:7], refs[7]
    copies = [pltpu.make_async_copy(a, b, sems.at[i]) for i, (a, b) in enumerate(zip(inputs, held))]
    for copy in copies:
        copy.start()
    state, step = held
    state_turned, step_same, step_opposite = outs
    side = place[4]
    for copy in copies:
        copy.wait()
    cols = state.shape[2]
    target = lax.broadcasted_iota(jnp.int32, (2 * cols, cols), 0)
    source = lax.broadcasted_iota(jnp.int32, (2 * cols, cols), 1)
    per = cols // G
    turned = 0.0
    for part in range(2):
        wanted = (source % G) * 2 * per + part * per + source // G
        turned = turned + lax.dot_general(
            (target == wanted).astype(BF16),
            state[:, part, :],
            (((1,), (1,)), ((), ())),
            preferred_element_type=F32,
        )
    state_turned[...] = turned.astype(BF16)
    half = step.shape[0] // 2
    turned_step = jnp.concatenate([step[...].astype(F32), jnp.zeros((PAD, step.shape[1]), F32)], axis=0)
    low = turned_step[:PAD]
    high = turned_step[half : half + PAD]
    step_same[...] = jnp.where(side == 0, low, high).astype(BF16)
    step_opposite[...] = jnp.where(side == 0, high, low).astype(BF16)


def settings_kernel(heads_mine, place, *refs):
    inputs, outs, held, sems = refs[:5], refs[5:12], refs[12:17], refs[17]
    copies = [pltpu.make_async_copy(a, b, sems.at[i]) for i, (a, b) in enumerate(zip(inputs, held))]
    for copy in copies:
        copy.start()
    project, taps, mixer_taps, step_bias, decay_log = held
    for copy in copies:
        copy.wait()
    gate_same, gate_opposite, gate_sent, taps_state, taps_mixer, bias, rate = outs
    quarter, core, side = place[0], place[3], place[4]
    width = gate_same.shape[1]
    other_side = 1 - side
    gate_same[...] = side_columns(project, 0, 2 * side + core, width)
    gate_opposite[...] = side_columns(project, 0, 2 * other_side + core, width)
    gate_sent[:, :width] = side_columns(project, 0, 2 * side + 1 - core, width)
    gate_sent[:, width:] = side_columns(project, 0, 2 * other_side + 1 - core, width)
    source = lax.broadcasted_iota(jnp.int32, (taps.shape[2], N), 0)
    target = lax.broadcasted_iota(jnp.int32, (taps.shape[2], N), 1)
    chosen = (source == target * G + place[5]).astype(F32)
    mine = jnp.where(core == 0, taps[:, 0, :], taps[:, 1, :])
    taps_state[: CONV + 1] = exact_dot(mine, chosen, ((1,), (0,)))
    if width % LANES == 0:
        taps_mixer[: CONV + 1] = mixer_taps[:, pl.ds(pl.multiple_of(quarter * width, width), width)]
    else:
        got = mixer_taps[:, :width]
        for k in range(1, TEAM):
            got = jnp.where(quarter == k, mixer_taps[:, k * width : (k + 1) * width], got)
        taps_mixer[: CONV + 1] = got
    heads = step_bias.shape[1]
    row = lax.broadcasted_iota(jnp.int32, (PAD, heads), 0)
    column = lax.broadcasted_iota(jnp.int32, (PAD, heads), 1)
    own = jnp.logical_and(column == quarter * heads_mine + row, row < heads_mine)
    for values, out in ((step_bias[...], bias), (-jnp.exp(decay_log[...]), rate)):
        picked = jnp.sum(jnp.where(own, values, 0.0), axis=1, keepdims=True)
        out[...] = jnp.broadcast_to(picked, out.shape)


def either_kernel(place, first, second, out, sem):
    for core, values in enumerate((first, second)):

        @pl.when(place[3] == core)
        def _():
            copy = pltpu.make_async_copy(values, out, sem)
            copy.start()
            copy.wait()


def partner_columns_kernel(place, *refs):
    pieces, out = refs[:-1], refs[-1]
    width = out.shape[2]
    other = 1 - place[3]
    for d, piece in enumerate(pieces):
        if width % LANES == 0:
            out[d] = piece[:, pl.ds(pl.multiple_of(other * width, width), width)]
        else:
            out[d] = jnp.where(other == 0, piece[:, :width], piece[:, width:])


def partner_rows_kernel(place, *refs):
    pieces, out = refs[:-1], refs[-1]
    other = pl.multiple_of((1 - place[3]) * N, N)
    for d, piece in enumerate(pieces):
        out[d, :N] = piece[pl.ds(other, N), :]
        out[d, N:] = piece[2 * N :, :]


def payload_kernel(place, turned, *refs):
    received, steps, outs = refs[:-4], refs[-4:-2], refs[-2:]
    inner_id = place[1]
    rows = turned.shape[0] // G
    part = rows // 2
    for d in range(len(received) + 1):
        piece = received[d - 1] if d else turned.at[pl.ds(pl.multiple_of(place[5] * rows, rows), rows)]
        for k in range(2):
            start = pl.multiple_of(k * N + (inner_id ^ d) * part, part)
            for out in outs:
                out[pl.ds(start, part), :] = piece[k * part : (k + 1) * part, :]
    for step, out in zip(steps, outs):
        out[2 * N :, :] = step[...]


def sent_kernel(group_of, place, turned, *outs):
    rows = turned.shape[0] // G
    for d, out in enumerate(outs):
        start = pl.multiple_of(group_of(place[1] ^ (d + 1)) * rows, rows)
        out[...] = turned[pl.ds(start, rows), :]


def assemble_kernel(heads_mine, place, sent, *refs):
    pieces, out = refs[:-1], refs[-1]
    z_id, core = place[2], place[3]
    rows = pieces[0].shape[1]
    for d, piece in enumerate(pieces):
        own = piece[pl.ds(pl.multiple_of(core * N, N), N), :]
        for m, (state, step) in enumerate(((own, piece[2 * N :, :]), (sent[d, :N, :], sent[d, N:, :]))):
            step = step.astype(F32)
            mine = jnp.where(core == 0, step[:heads_mine], step[heads_mine : 2 * heads_mine])
            packed = jnp.concatenate(
                [state.astype(F32), mine, jnp.zeros((LANES - heads_mine, rows), F32)], axis=0
            )
            row = pl.multiple_of((2 * (z_id ^ d) + (core ^ m)) * rows, rows)
            out[pl.ds(row, rows), :] = packed.T.astype(BF16)


def tail_kernel(place, *refs):
    blocks, out, sem = refs[:-2], refs[-2], refs[-1]
    inner_count = len(blocks) // 2
    for d, block in enumerate(blocks):
        away, di = d // inner_count, d % inner_count

        @pl.when(jnp.logical_and(place[3] == 1 - away, place[1] == (inner_count - 1) ^ di))
        def _():
            copy = pltpu.make_async_copy(block.at[pl.ds(block.shape[0] - HALO, HALO)], out, sem)
            copy.start()
            copy.wait()


def fetch_blocks(place, blocks, scratch, sems, inner_count, offset):
    inner_id = place[1]
    rows = blocks[0].shape[0]
    copies = []
    for d, block in enumerate(blocks):
        j, di = d // inner_count, d % inner_count
        row = pl.multiple_of(offset + j * inner_count * rows + (inner_id ^ di) * rows, HALO)
        copies.append(pltpu.make_async_copy(block, scratch.at[pl.ds(row, rows)], sems.at[d]))
    for copy in copies:
        copy.start()
    return copies


def wide_dot(a, b):
    return jnp.dot(a, b, preferred_element_type=F32)


def exact_dot(a, b, dims):
    return lax.dot_general(a, b, (dims, ((), ())), precision=lax.Precision.HIGHEST, preferred_element_type=F32)


def convolved(pre, taps, block):
    window = pre[pl.ds(pl.multiple_of(block * SPAN, SPAN), SPAN + HALO), :].astype(F32)
    start = HALO - (CONV - 1)
    mixed = taps[CONV : CONV + 1, :] + taps[0:1, :] * window[start : start + SPAN]
    for k in range(1, CONV):
        mixed = mixed + taps[k : k + 1, :] * window[start + k : start + k + SPAN]
    return mixed / (1.0 + jnp.exp(-mixed))


def spread(width):
    row = lax.broadcasted_iota(jnp.int32, (PAD, width), 0)
    column = lax.broadcasted_iota(jnp.int32, (PAD, width), 1)
    return (column // P_SIZE == row).astype(F32)


def projected(place, source, parts, tok, weight, sems, wsems, inner_count, keep):
    waits = fetch_weights(place, parts, weight, wsems) if parts else []
    blocks = source[:-1]
    span = (tok.shape[0] - HALO) // TEAM
    copies = []
    if blocks:
        top = pltpu.make_async_copy(source[-1], tok.at[pl.ds(0, HALO)], sems.at[len(blocks)])
        top.start()
        copies = fetch_blocks(place, blocks, tok, sems, inner_count, HALO)
        waits = waits + [top]
    for copy in waits:
        copy.wait()
    for j in range(TEAM):
        for di in range(inner_count if blocks else 0):
            copies[j * inner_count + di].wait()
        first = 0 if j == 0 else HALO + j * span
        size = span + (HALO if j == 0 else 0)
        keep(wide_dot(tok[pl.ds(first, size), :], weight[...]), j)


def state_kernel(inner_count, place, taps, bias, rate, weight, *refs):
    source, refs = refs[:-6], refs[-6:]
    half_out, step_out, cum_out, tok, pre, sems = refs
    span = (tok.shape[0] - HALO) // TEAM
    quarter = place[0]

    def keep(result, j):
        if j == 0:
            pre[pl.ds(0, HALO), :] = result[:HALO, :N].astype(BF16)
            result = result[HALO:]
        whose = quarter ^ j
        pre[pl.ds(pl.multiple_of(HALO + whose * span, HALO), span), :] = result[:, :N].astype(BF16)
        raw = result[:, N:].astype(BF16).astype(F32)
        for b in range(span // SPAN):
            turned = raw[b * SPAN : (b + 1) * SPAN].T
            step_out[whose * (span // SPAN) + b] = turned[:PAD]

    projected(place, source, (), tok, weight, sems, None, inner_count, keep)

    total = step_out.shape[0] * PAD
    raw = step_out[...] + bias[...][None]
    step = jnp.maximum(raw, 0.0) + jnp.log1p(jnp.exp(-jnp.abs(raw)))
    step_out[...] = step
    logdec = (step * rate[...][None]).reshape(total, SPAN)
    row = lax.broadcasted_iota(jnp.int32, (SPAN, SPAN), 0)
    column = lax.broadcasted_iota(jnp.int32, (SPAN, SPAN), 1)
    upper = (row <= column).astype(F32)
    cum_out[...] = exact_dot(logdec, upper, ((1,), (0,))).reshape(step_out.shape)

    def one(p, _):
        half_out[pl.ds(pl.multiple_of(p * SPAN, SPAN), SPAN), :] = convolved(pre, taps, p).astype(BF16)
        return 0

    lax.fori_loop(0, step_out.shape[0], one, 0, unroll=2)


def mixer_kernel(inner_count, shared, z_count, place, taps, half, half_other, step, cum, other, *refs):
    pieces, refs = refs[:z_count], refs[z_count:]
    tail = 8 if shared else 9
    source, refs = refs[:-tail], refs[-tail:]
    if shared:
        tok, source = source[0], ()
        x_out, states_out, last_out, through_out, weight, pre, sems, wsems = refs
        source = (None,)
    else:
        x_out, states_out, last_out, through_out, tok, weight, pre, sems, wsems = refs
    span = (tok.shape[0] - HALO) // TEAM
    quarter, core = place[0], place[3]
    width = x_out.shape[1]
    parts = []
    for d, piece in enumerate(pieces):
        view = piece
        if piece.shape[1] != width:
            view = piece.at[:, pl.ds(pl.multiple_of(core * width, width), width)]
        parts += [(view, d, 0), (other.at[d], d, 1)]

    def keep(result, j):
        if j == 0:
            pre[pl.ds(0, HALO), :] = result[:HALO].astype(BF16)
            result = result[HALO:]
        whose = quarter ^ j
        pre[pl.ds(pl.multiple_of(HALO + whose * span, HALO), span), :] = result.astype(BF16)

    projected(place, source, parts, tok, weight, sems, wsems, inner_count, keep)
    heads = spread(width)

    def one(p, carry):
        state, log_sum = carry
        rows = pl.ds(pl.multiple_of(p * SPAN, SPAN), SPAN)
        x = convolved(pre, taps, p).astype(BF16)
        x_out[rows, :] = x
        states_out[p] = state
        cum_p = cum[p]
        ends = cum_p[:, SPAN - 1 :]
        to_end = jnp.exp(ends - cum_p) * step[p]
        scaled = (x.astype(F32) * exact_dot(to_end, heads, ((0,), (0,)))).astype(BF16)
        b = jnp.where(core == 0, half[rows, :], half_other[rows, :])
        fresh = lax.dot_general(b, scaled, (((0,), (0,)), ((), ())), preferred_element_type=F32)
        end_row = jnp.sum(ends * heads, axis=0, keepdims=True)
        return jnp.exp(end_row) * state + fresh, log_sum + end_row

    state, log_sum = lax.fori_loop(
        0, step.shape[0], one, (jnp.zeros((N, width), F32), jnp.zeros((1, width), F32)), unroll=2
    )
    last_out[...] = state.astype(BF16)
    through_out[...] = jnp.broadcast_to(jnp.exp(log_sum), through_out.shape)


def gate_kernel(inner_count, shared, z_count, place, *refs):
    pieces, refs = refs[:z_count], refs[z_count:]
    tail = 4 if shared else 5
    source, refs = refs[:-tail], refs[-tail:]
    if shared:
        tok = source[0]
        source = (None,)
        gate_out, weight, sems, wsems = refs
    else:
        gate_out, tok, weight, sems, wsems = refs
    span = (tok.shape[0] - HALO) // TEAM
    quarter = place[0]
    parts = []
    for d, piece in enumerate(pieces):
        rows = piece.shape[0] // 2
        parts += [(piece.at[pl.ds(m * rows, rows)], d, m) for m in range(2)]

    def keep(result, j):
        result = result[HALO:] if j == 0 else result
        gate_out[pl.ds(pl.multiple_of((quarter ^ j) * span, span), span), :] = result.astype(BF16)

    projected(place, source, parts, tok, weight, sems, wsems, inner_count, keep)


def scan_kernel(place, half, half_other, x_vals, gate, step, cum, states, prior, gated_out):
    width = x_vals.shape[1]
    heads_mine = width // P_SIZE
    heads = spread(width)
    core = place[3]
    lane = lax.broadcasted_iota(jnp.int32, (SPAN, width), 1) // P_SIZE
    row = lax.broadcasted_iota(jnp.int32, (SPAN, SPAN), 0)
    column = lax.broadcasted_iota(jnp.int32, (SPAN, SPAN), 1)
    lower = column <= row
    entering = prior[...].astype(F32)

    def one(p, before):
        rows = pl.ds(pl.multiple_of(p * SPAN, SPAN), SPAN)
        first, second = half[rows, :], half_other[rows, :]
        b = jnp.where(core == 0, first, second)
        c = jnp.where(core == 0, second, first)
        x = x_vals[rows, :]
        cum_p = cum[p]
        step_p = step[p]
        scores = lax.dot_general(
            c, b, (((1,), (1,)), ((), ())), preferred_element_type=F32
        )
        cum_t = cum_p.T
        mixes = []
        parts = []
        for h in range(heads_mine):
            spacing = jnp.where(lower, cum_t[:, h : h + 1] - cum_p[h : h + 1, :], -jnp.inf)
            mixes.append((scores * jnp.exp(spacing) * step_p[h : h + 1, :]).astype(BF16))
            parts.append(jnp.where(lane == h, x, jnp.zeros_like(x)))
        diagonal = wide_dot(jnp.concatenate(mixes, axis=1), jnp.concatenate(parts, axis=0))
        state = states[p] + jnp.exp(before) * entering
        decay = exact_dot(jnp.exp(cum_p), heads, ((0,), (0,)))
        y = diagonal + decay * wide_dot(c, state.astype(BF16))
        g = gate[rows, :].astype(F32)
        gated_out[rows, :] = (y * (g / (1.0 + jnp.exp(-g)))).astype(BF16)
        return before + jnp.sum(cum_p[:, SPAN - 1 :] * heads, axis=0, keepdims=True)

    lax.fori_loop(0, step.shape[0], one, jnp.zeros((1, width), F32), unroll=2)


def norm_kernel(inner_count, parts, gain, out):
    width = parts.shape[2]
    group_width = H * P_SIZE // G
    for g in range(G):
        members = []
        power = 0.0
        for c in range(g * group_width, (g + 1) * group_width, width):
            index = c // width
            i, k = index // TEAM, index % TEAM
            wide = parts[k * inner_count + i].astype(F32)
            members.append((c, wide))
            power = power + jnp.sum(wide * wide, axis=1, keepdims=True)
        scale = lax.rsqrt(power / group_width + EPSILON)
        for c, wide in members:
            out[:, c : c + width] = (wide * scale * gain[:, c : c + width]).astype(BF16)


def on_device(
    tokens,
    project_weight,
    state_weight,
    step_weight,
    mixer_taps,
    state_taps,
    step_bias,
    decay_log,
    norm_gain,
):
    ctx_count = lax.axis_size("ctx")
    inner_count = lax.axis_size("inner")
    z_count = ctx_count // 2
    members = TEAM * inner_count

    rows_here, _, width_here = project_weight.shape
    row_count, model_width = tokens.shape
    heads_here = step_weight.shape[1]
    heads_mine = heads_here // TEAM
    width_mine = width_here // TEAM
    per_group = H // G
    spread_out = heads_here // per_group, per_group // heads_here

    def at(kernel):
        return lambda *refs: kernel(here(*spread_out), *refs)

    total = members * row_count
    count = total // SPAN

    def sds(shape, dtype):
        return jax.ShapeDtypeStruct(shape, dtype)

    partner = swapped(tokens, "ctx", 2)
    near = inner_blocks(tokens, at, inner_count, ctx_count)
    beyond = inner_blocks(partner, at, inner_count, ctx_count)
    blocks = (
        near
        + [swapped(b, "ctx", 1) for b in near]
        + beyond
        + [swapped(b, "ctx", 1) for b in beyond]
    )
    tail = pl.pallas_call(
        at(tail_kernel),
        in_specs=[ANY] * (2 * inner_count),
        out_specs=VMEM,
        out_shape=sds((HALO, model_width), BF16),
        scratch_shapes=[pltpu.SemaphoreType.DMA],
        compiler_params=SMALL,
        name="tail",
    )(*blocks[: 2 * inner_count])
    halo = jnp.zeros_like(tail)
    for k in range(2):
        pairs = [
            (c - 2 + m, c + 2 * k + m) for c in range(TEAM, ctx_count, TEAM) for m in range(2)
        ]
        halo = halo + lax.ppermute(tail, "ctx", pairs)

    pair = 2 * width_mine
    slice_cols = state_weight.shape[2]
    chunks = 4
    x_sides = pl.pallas_call(
        at(mixer_columns_kernel),
        in_specs=[HBM],
        out_specs=[VMEM] * 2,
        out_shape=[sds((rows_here, pair), BF16)] * 2,
        scratch_shapes=[
            pltpu.VMEM((chunks, rows_here // chunks, 2, width_here), BF16),
            pltpu.SemaphoreType.DMA((chunks,)),
        ],
        compiler_params=SMALL,
        name="columns",
    )(project_weight)

    def held_in_vmem(values):
        return [pltpu.VMEM(v.shape, v.dtype) for v in values] + [pltpu.SemaphoreType.DMA((len(values),))]

    to_prepare = (state_weight, step_weight.T)
    state_turned, *step_sides = pl.pallas_call(
        at(prepare_kernel),
        in_specs=[HBM] * 2,
        out_specs=[VMEM] * 3,
        out_shape=[
            sds((2 * slice_cols, rows_here), BF16),
            sds((PAD, rows_here), BF16),
            sds((PAD, rows_here), BF16),
        ],
        scratch_shapes=held_in_vmem(to_prepare),
        compiler_params=SMALL,
        name="prepare",
    )(*to_prepare)
    to_set = (
        project_weight,
        state_taps,
        mixer_taps,
        step_bias.reshape(1, -1),
        decay_log.reshape(1, -1),
    )
    settings = pl.pallas_call(
        at(functools.partial(settings_kernel, heads_mine)),
        in_specs=[HBM] * 5,
        out_specs=[VMEM] * 7,
        out_shape=[
            sds((rows_here, width_mine), BF16),
            sds((rows_here, width_mine), BF16),
            sds((rows_here, pair), BF16),
            sds((PAD, N), F32),
            sds((PAD, width_mine), F32),
            sds((PAD, SPAN), F32),
            sds((PAD, SPAN), F32),
        ],
        scratch_shapes=held_in_vmem(to_set),
        compiler_params=SMALL,
        name="settings",
    )(*to_set)
    gate_mine, gate_sent = settings[:2], settings[2]

    x_pieces = gathered_rows(lambda d: x_sides[d % 2], z_count)

    def of_core(piece, which):
        return lax.dynamic_slice_in_dim(piece, which * width_mine, width_mine, 1)

    x_sent = pl.pallas_call(
        at(partner_columns_kernel),
        in_specs=[VMEM] * z_count,
        out_specs=VMEM,
        out_shape=sds((z_count, rows_here, width_mine), BF16),
        compiler_params=SMALL,
        name="xsplit",
    )(*x_pieces)
    x_other = swapped(x_sent, "ctx", 1)
    if width_mine % LANES:
        x_pieces = [of_core(p, lax.axis_index("ctx") % 2) for p in x_pieces]

    part_rows = 2 * slice_cols // G
    if part_rows % (2 * HALO) == 0:
        sent = pl.pallas_call(
            at(functools.partial(sent_kernel, lambda j: group_of(j, *spread_out))),
            in_specs=[VMEM],
            out_specs=[VMEM] * (inner_count - 1),
            out_shape=[sds((part_rows, rows_here), BF16)] * (inner_count - 1),
            compiler_params=SMALL,
            name="sent",
        )(state_turned)
        received = [swapped(sent[d - 1], "inner", d) for d in range(1, inner_count)]
        payload_call = pl.pallas_call(
            at(payload_kernel),
            in_specs=[VMEM] * (inner_count + 2),
            out_specs=[VMEM] * 2,
            out_shape=[sds((2 * N + PAD, rows_here), BF16)] * 2,
            compiler_params=SMALL,
            name="payload",
        )
        payloads = payload_call(state_turned, *received, *step_sides)
    else:
        to_each = jnp.concatenate(
            [
                lax.slice_in_dim(state_turned, g * part_rows, (g + 1) * part_rows, axis=0)
                for g in [(j * heads_here) // per_group for j in range(inner_count)]
            ],
            axis=0,
        ).reshape(inner_count, part_rows, rows_here)
        state_rows = lax.all_to_all(to_each, "inner", 0, 0, tiled=True)
        state_rows = state_rows.reshape(inner_count, 2, part_rows // 2, rows_here)
        state_rows = state_rows.transpose(1, 0, 2, 3).reshape(2 * N, rows_here)
        payloads = [jnp.concatenate([state_rows, s], axis=0) for s in step_sides]
    state_pieces = gathered_rows(lambda d: payloads[d % 2], z_count)
    state_sent = pl.pallas_call(
        at(partner_rows_kernel),
        in_specs=[VMEM] * z_count,
        out_specs=VMEM,
        out_shape=sds((z_count, N + PAD, rows_here), BF16),
        compiler_params=SMALL,
        name="ssplit",
    )(*state_pieces)
    state_other = swapped(state_sent, "ctx", 1)
    state_matrix = pl.pallas_call(
        at(functools.partial(assemble_kernel, heads_mine)),
        in_specs=[VMEM] * (1 + z_count),
        out_specs=VMEM,
        out_shape=sds((model_width, N + LANES), BF16),
        compiler_params=SMALL,
        name="assemble",
    )(state_other, *state_pieces)

    gate_other = swapped(gate_sent, "ctx", 1)
    gate_chip = [
        jnp.concatenate([gate_mine[s], gate_other[:, s * width_mine : (s + 1) * width_mine]], axis=0)
        for s in range(2)
    ]
    gate_pieces = gathered_rows(lambda d: gate_chip[d % 2], z_count)

    taps_state, taps_mine, bias_mine, rate_mine = settings[3:]

    shared = total * model_width <= 2**23
    tok_shape = (HALO + total, model_width)
    held = 2 * tok_shape[0] * model_width
    limit = pltpu.CompilerParams(vmem_limit_bytes=min(60 << 20, held + (4 << 20 if shared else 22 << 20)))

    def scratch(width, pre_width, own_tok):
        made = [pltpu.VMEM(tok_shape, BF16)] if own_tok else []
        if width:
            made.append(pltpu.VMEM((model_width, width), BF16))
        if pre_width:
            made.append(pltpu.VMEM((HALO + total, pre_width), BF16))
        return made + [pltpu.SemaphoreType.DMA((members + 1,)), pltpu.SemaphoreType.DMA((2 * z_count,))]

    source = list(blocks) + [halo]
    any_of = lambda values: [ANY] * len(values)
    state_outs = [sds((total, N), BF16), sds((count, PAD, SPAN), F32), sds((count, PAD, SPAN), F32)]
    outs = pl.pallas_call(
        at(functools.partial(state_kernel, inner_count)),
        in_specs=[VMEM] * 4 + any_of(source),
        out_specs=[VMEM] * (4 if shared else 3),
        out_shape=state_outs + ([sds(tok_shape, BF16)] if shared else []),
        scratch_shapes=scratch(0, N, not shared)[:-1],
        compiler_params=limit,
        name="state",
    )(taps_state, bias_mine, rate_mine, state_matrix, *source)
    half, step, cum = outs[:3]
    if shared:
        source = [outs[3]]
    held_spec = [VMEM] if shared else any_of(source)
    half_other = swapped(half, "ctx", 1)

    x_vals, states, last_state, through = pl.pallas_call(
        at(functools.partial(mixer_kernel, inner_count, shared, z_count)),
        in_specs=[VMEM] * 5 + [ANY] + any_of(x_pieces) + held_spec,
        out_specs=[VMEM, VMEM, VMEM, VMEM],
        out_shape=[
            sds((total, width_mine), BF16),
            sds((count, N, width_mine), F32),
            sds((N, width_mine), BF16),
            sds((PAD, width_mine), F32),
        ],
        scratch_shapes=scratch(width_mine, width_mine, not shared),
        compiler_params=limit,
        name="mixer",
    )(taps_mine, half, half_other, step, cum, x_other, *x_pieces, *source)

    hops = ctx_count // TEAM - 1
    pairs = [(c, c + TEAM) for c in range(ctx_count - TEAM)]
    prior = jnp.zeros_like(last_state)
    for hop in range(hops):
        sent = last_state
        if hop:
            sent = (through[:1] * prior.astype(F32) + last_state.astype(F32)).astype(BF16)
        prior = lax.ppermute(sent, "ctx", pairs)

    gate_values = pl.pallas_call(
        at(functools.partial(gate_kernel, inner_count, shared, z_count)),
        in_specs=any_of(gate_pieces) + held_spec,
        out_specs=VMEM,
        out_shape=sds((total, width_mine), BF16),
        scratch_shapes=scratch(width_mine, 0, not shared),
        compiler_params=limit,
        name="gate",
    )(*gate_pieces, *source)

    gated = pl.pallas_call(
        at(scan_kernel),
        in_specs=[VMEM] * 8,
        out_specs=VMEM,
        out_shape=sds((total, width_mine), BF16),
        compiler_params=limit,
        name="scan",
    )(half, half_other, x_vals, gate_values, step, cum, states, prior)

    teams = [[t * members + m for m in range(members)] for t in range(ctx_count // TEAM)]
    parts = lax.all_to_all(
        gated, ("ctx", "inner"), 0, 0, axis_index_groups=teams, tiled=True
    ).reshape(members, row_count, width_mine)
    return pl.pallas_call(
        lambda *refs: norm_kernel(inner_count, *refs),
        in_specs=[VMEM, VMEM],
        out_specs=VMEM,
        out_shape=sds((row_count, H * P_SIZE), BF16),
        compiler_params=limit,
        name="norm",
    )(parts, norm_gain.reshape(1, -1))


def solution(mesh):
    placed = (
        P(("ctx", "inner"), None),
        P("ctx", None, "inner"),
        P("ctx", None, "inner"),
        P("ctx", "inner"),
        P(None, "inner"),
        P(),
        P("inner"),
        P("inner"),
        P(),
    )

    return jax.shard_map(
        on_device, mesh=mesh, in_specs=placed, out_specs=P(("ctx", "inner"), None), check_vma=False
    )
```

```python
import functools

import jax
import jax.numpy as jnp
from jax import lax
from jax.experimental import pallas as pl
from jax.experimental.pallas import tpu as pltpu
from jax.sharding import PartitionSpec as P


H = 64
P_SIZE = 64
N = 128
G = 4
CONV = 4
SPAN = 128
TEAM = 4
HALO = 16
LANES = 128
PAD = 8

EPSILON = 1e-05


ANY = pl.BlockSpec(memory_space=pl.ANY)
HBM = pl.BlockSpec(memory_space=pltpu.HBM)
VMEM = pl.BlockSpec(memory_space=pltpu.VMEM)
SMALL = pltpu.CompilerParams(vmem_limit_bytes=6 << 20)
F32 = jnp.float32
BF16 = jnp.bfloat16


def group_of(inner_id, heads_over, members_over):
    return inner_id * heads_over if heads_over else lax.div(inner_id, members_over)


def here(heads_over, members_over):
    ctx_id = lax.axis_index("ctx")
    inner_id = lax.axis_index("inner")
    z_id = lax.shift_right_logical(ctx_id, 1)
    return (
        ctx_id & (TEAM - 1),
        inner_id,
        z_id,
        ctx_id & 1,
        z_id & 1,
        group_of(inner_id, heads_over, members_over),
    )


def swapped(x, axis, mask):
    pairs = [(i, i ^ mask) for i in range(lax.axis_size(axis))]
    return lax.ppermute(x, axis, pairs)


def inner_blocks(block, at, inner_count, ctx_count):
    if inner_count != 4:
        got = [block]
        step = 1
        while step < inner_count:
            got = got + [swapped(b, "inner", step) for b in got]
            step *= 2
        return got
    near_x = swapped(block, "inner", 1)
    near_y = swapped(block, "inner", 2)
    pairs = []
    for c in range(ctx_count):
        for i in range(inner_count):
            pairs.append((c * inner_count + i, c * inner_count + (i ^ (1 if c % 2 else 2))))
    onward = pl.pallas_call(
        at(either_kernel),
        in_specs=[ANY, ANY],
        out_specs=VMEM,
        out_shape=jax.ShapeDtypeStruct(block.shape, block.dtype),
        scratch_shapes=[pltpu.SemaphoreType.DMA],
        compiler_params=SMALL,
        name="either",
    )(near_x, near_y)
    far = lax.ppermute(onward, ("ctx", "inner"), pairs)
    return [block, near_x, near_y, far]


def gathered_rows(piece_of, z_count):
    return [piece_of(d) if d == 0 else swapped(piece_of(d), "ctx", 2 * d) for d in range(z_count)]


def fetch_weights(place, parts, scratch, sems):
    z_id, core = place[2], place[3]
    copies = []
    for index, (view, d, m) in enumerate(parts):
        rows = view.shape[0]
        row = pl.multiple_of((2 * (z_id ^ d) + (core ^ m)) * rows, rows)
        copies.append(pltpu.make_async_copy(view, scratch.at[pl.ds(row, rows)], sems.at[index]))
    for copy in copies:
        copy.start()
    return copies


def side_columns(project, kind, index, size):
    if size % LANES == 0:
        return project[:, kind, pl.ds(pl.multiple_of(index * size, size), size)]
    got = project[:, kind, :size]
    for k in range(1, project.shape[2] // size):
        got = jnp.where(index == k, project[:, kind, k * size : (k + 1) * size], got)
    return got


def mixer_columns_kernel(place, project, same, opposite, held, sems):
    chunks = held.shape[0]
    rows = held.shape[1]
    pair = same.shape[1]
    copies = [
        pltpu.make_async_copy(project.at[pl.ds(c * rows, rows)], held.at[c], sems.at[c]) for c in range(chunks)
    ]
    for copy in copies:
        copy.start()
    for c, copy in enumerate(copies):
        copy.wait()
        same[c * rows : (c + 1) * rows] = side_columns(held.at[c], 1, place[4], pair)
        opposite[c * rows : (c + 1) * rows] = side_columns(held.at[c], 1, 1 - place[4], pair)


def prepare_kernel(place, *refs):
    inputs, outs, held, sems = refs[:2], refs[2:5], refs[5:7], refs[7]
    copies = [pltpu.make_async_copy(a, b, sems.at[i]) for i, (a, b) in enumerate(zip(inputs, held))]
    for copy in copies:
        copy.start()
    state, step = held
    state_turned, step_same, step_opposite = outs
    side = place[4]
    for copy in copies:
        copy.wait()
    cols = state.shape[2]
    target = lax.broadcasted_iota(jnp.int32, (2 * cols, cols), 0)
    source = lax.broadcasted_iota(jnp.int32, (2 * cols, cols), 1)
    per = cols // G
    turned = 0.0
    for part in range(2):
        wanted = (source % G) * 2 * per + part * per + source // G
        turned = turned + lax.dot_general(
            (target == wanted).astype(BF16),
            state[:, part, :],
            (((1,), (1,)), ((), ())),
            preferred_element_type=F32,
        )
    state_turned[...] = turned.astype(BF16)
    half = step.shape[0] // 2
    turned_step = jnp.concatenate([step[...].astype(F32), jnp.zeros((PAD, step.shape[1]), F32)], axis=0)
    low = turned_step[:PAD]
    high = turned_step[half : half + PAD]
    step_same[...] = jnp.where(side == 0, low, high).astype(BF16)
    step_opposite[...] = jnp.where(side == 0, high, low).astype(BF16)


def settings_kernel(heads_mine, place, *refs):
    inputs, outs, held, sems = refs[:5], refs[5:12], refs[12:17], refs[17]
    copies = [pltpu.make_async_copy(a, b, sems.at[i]) for i, (a, b) in enumerate(zip(inputs, held))]
    for copy in copies:
        copy.start()
    project, taps, mixer_taps, step_bias, decay_log = held
    for copy in copies:
        copy.wait()
    gate_same, gate_opposite, gate_sent, taps_state, taps_mixer, bias, rate = outs
    quarter, core, side = place[0], place[3], place[4]
    width = gate_same.shape[1]
    other_side = 1 - side
    gate_same[...] = side_columns(project, 0, 2 * side + core, width)
    gate_opposite[...] = side_columns(project, 0, 2 * other_side + core, width)
    gate_sent[:, :width] = side_columns(project, 0, 2 * side + 1 - core, width)
    gate_sent[:, width:] = side_columns(project, 0, 2 * other_side + 1 - core, width)
    source = lax.broadcasted_iota(jnp.int32, (taps.shape[2], N), 0)
    target = lax.broadcasted_iota(jnp.int32, (taps.shape[2], N), 1)
    chosen = (source == target * G + place[5]).astype(F32)
    mine = jnp.where(core == 0, taps[:, 0, :], taps[:, 1, :])
    taps_state[: CONV + 1] = exact_dot(mine, chosen, ((1,), (0,)))
    if width % LANES == 0:
        taps_mixer[: CONV + 1] = mixer_taps[:, pl.ds(pl.multiple_of(quarter * width, width), width)]
    else:
        got = mixer_taps[:, :width]
        for k in range(1, TEAM):
            got = jnp.where(quarter == k, mixer_taps[:, k * width : (k + 1) * width], got)
        taps_mixer[: CONV + 1] = got
    heads = step_bias.shape[1]
    row = lax.broadcasted_iota(jnp.int32, (PAD, heads), 0)
    column = lax.broadcasted_iota(jnp.int32, (PAD, heads), 1)
    own = jnp.logical_and(column == quarter * heads_mine + row, row < heads_mine)
    for values, out in ((step_bias[...], bias), (-jnp.exp(decay_log[...]), rate)):
        picked = jnp.sum(jnp.where(own, values, 0.0), axis=1, keepdims=True)
        out[...] = jnp.broadcast_to(picked, out.shape)


def either_kernel(place, first, second, out, sem):
    for core, values in enumerate((first, second)):

        @pl.when(place[3] == core)
        def _():
            copy = pltpu.make_async_copy(values, out, sem)
            copy.start()
            copy.wait()


def partner_columns_kernel(place, *refs):
    pieces, out = refs[:-1], refs[-1]
    width = out.shape[2]
    other = 1 - place[3]
    for d, piece in enumerate(pieces):
        if width % LANES == 0:
            out[d] = piece[:, pl.ds(pl.multiple_of(other * width, width), width)]
        else:
            out[d] = jnp.where(other == 0, piece[:, :width], piece[:, width:])


def partner_rows_kernel(place, *refs):
    pieces, out = refs[:-1], refs[-1]
    other = pl.multiple_of((1 - place[3]) * N, N)
    for d, piece in enumerate(pieces):
        out[d, :N] = piece[pl.ds(other, N), :]
        out[d, N:] = piece[2 * N :, :]


def payload_kernel(place, turned, *refs):
    received, steps, outs = refs[:-4], refs[-4:-2], refs[-2:]
    inner_id = place[1]
    rows = turned.shape[0] // G
    part = rows // 2
    for d in range(len(received) + 1):
        piece = received[d - 1] if d else turned.at[pl.ds(pl.multiple_of(place[5] * rows, rows), rows)]
        for k in range(2):
            start = pl.multiple_of(k * N + (inner_id ^ d) * part, part)
            for out in outs:
                out[pl.ds(start, part), :] = piece[k * part : (k + 1) * part, :]
    for step, out in zip(steps, outs):
        out[2 * N :, :] = step[...]


def sent_kernel(group_of, place, turned, *outs):
    rows = turned.shape[0] // G
    for d, out in enumerate(outs):
        start = pl.multiple_of(group_of(place[1] ^ (d + 1)) * rows, rows)
        out[...] = turned[pl.ds(start, rows), :]


def assemble_kernel(heads_mine, place, sent, *refs):
    pieces, out = refs[:-1], refs[-1]
    z_id, core = place[2], place[3]
    rows = pieces[0].shape[1]
    for d, piece in enumerate(pieces):
        own = piece[pl.ds(pl.multiple_of(core * N, N), N), :]
        for m, (state, step) in enumerate(((own, piece[2 * N :, :]), (sent[d, :N, :], sent[d, N:, :]))):
            step = step.astype(F32)
            mine = jnp.where(core == 0, step[:heads_mine], step[heads_mine : 2 * heads_mine])
            packed = jnp.concatenate(
                [state.astype(F32), mine, jnp.zeros((LANES - heads_mine, rows), F32)], axis=0
            )
            row = pl.multiple_of((2 * (z_id ^ d) + (core ^ m)) * rows, rows)
            out[pl.ds(row, rows), :] = packed.T.astype(BF16)


def tail_kernel(place, *refs):
    blocks, out, sem = refs[:-2], refs[-2], refs[-1]
    inner_count = len(blocks) // 2
    for d, block in enumerate(blocks):
        away, di = d // inner_count, d % inner_count

        @pl.when(jnp.logical_and(place[3] == 1 - away, place[1] == (inner_count - 1) ^ di))
        def _():
            copy = pltpu.make_async_copy(block.at[pl.ds(block.shape[0] - HALO, HALO)], out, sem)
            copy.start()
            copy.wait()


def fetch_blocks(place, blocks, scratch, sems, inner_count, offset):
    inner_id = place[1]
    rows = blocks[0].shape[0]
    copies = []
    for d, block in enumerate(blocks):
        j, di = d // inner_count, d % inner_count
        row = pl.multiple_of(offset + j * inner_count * rows + (inner_id ^ di) * rows, HALO)
        copies.append(pltpu.make_async_copy(block, scratch.at[pl.ds(row, rows)], sems.at[d]))
    for copy in copies:
        copy.start()
    return copies


def wide_dot(a, b):
    return jnp.dot(a, b, preferred_element_type=F32)


def exact_dot(a, b, dims):
    return lax.dot_general(a, b, (dims, ((), ())), precision=lax.Precision.HIGHEST, preferred_element_type=F32)


def convolved(pre, taps, block):
    window = pre[pl.ds(pl.multiple_of(block * SPAN, SPAN), SPAN + HALO), :].astype(F32)
    start = HALO - (CONV - 1)
    mixed = taps[CONV : CONV + 1, :] + taps[0:1, :] * window[start : start + SPAN]
    for k in range(1, CONV):
        mixed = mixed + taps[k : k + 1, :] * window[start + k : start + k + SPAN]
    return mixed / (1.0 + jnp.exp(-mixed))


def three_parts(values):
    high = values.astype(BF16)
    rest = values - high.astype(F32)
    middle = rest.astype(BF16)
    low = (rest - middle.astype(F32)).astype(BF16)
    return high, middle, low


def over_lanes(by_head, heads):
    return lax.dot_general(
        jnp.concatenate(three_parts(by_head), axis=0),
        jnp.concatenate([heads] * 3, axis=0).astype(BF16),
        (((0,), (0,)), ((), ())),
        preferred_element_type=F32,
    )


def spread(width):
    row = lax.broadcasted_iota(jnp.int32, (PAD, width), 0)
    column = lax.broadcasted_iota(jnp.int32, (PAD, width), 1)
    return (column // P_SIZE == row).astype(F32)


def projected(place, source, parts, tok, weight, sems, wsems, inner_count, keep):
    waits = fetch_weights(place, parts, weight, wsems) if parts else []
    blocks = source[:-1]
    span = (tok.shape[0] - HALO) // TEAM
    copies = []
    if blocks:
        top = pltpu.make_async_copy(source[-1], tok.at[pl.ds(0, HALO)], sems.at[len(blocks)])
        top.start()
        copies = fetch_blocks(place, blocks, tok, sems, inner_count, HALO)
        waits = waits + [top]
    for copy in waits:
        copy.wait()
    for j in range(TEAM):
        for di in range(inner_count if blocks else 0):
            copies[j * inner_count + di].wait()
        first = 0 if j == 0 else HALO + j * span
        size = span + (HALO if j == 0 else 0)
        keep(wide_dot(tok[pl.ds(first, size), :], weight[...]), j)


def state_kernel(inner_count, place, taps, bias, rate, weight, *refs):
    source, refs = refs[:-6], refs[-6:]
    half_out, step_out, cum_out, tok, pre, sems = refs
    span = (tok.shape[0] - HALO) // TEAM
    quarter = place[0]

    def keep(result, j):
        if j == 0:
            pre[pl.ds(0, HALO), :] = result[:HALO, :N].astype(BF16)
            result = result[HALO:]
        whose = quarter ^ j
        pre[pl.ds(pl.multiple_of(HALO + whose * span, HALO), span), :] = result[:, :N].astype(BF16)
        raw = result[:, N:].astype(BF16).astype(F32)
        for b in range(span // SPAN):
            turned = raw[b * SPAN : (b + 1) * SPAN].T
            step_out[whose * (span // SPAN) + b] = turned[:PAD]

    projected(place, source, (), tok, weight, sems, None, inner_count, keep)

    total = step_out.shape[0] * PAD
    raw = step_out[...] + bias[...][None]
    step = jnp.maximum(raw, 0.0) + jnp.log1p(jnp.exp(-jnp.abs(raw)))
    step_out[...] = step
    logdec = (step * rate[...][None]).reshape(total, SPAN)
    row = lax.broadcasted_iota(jnp.int32, (SPAN, SPAN), 0)
    column = lax.broadcasted_iota(jnp.int32, (SPAN, SPAN), 1)
    upper = (row <= column).astype(BF16)
    parts = jnp.concatenate(three_parts(logdec), axis=1)
    cum_out[...] = wide_dot(parts, jnp.concatenate([upper] * 3, axis=0)).reshape(step_out.shape)

    def one(p, _):
        half_out[pl.ds(pl.multiple_of(p * SPAN, SPAN), SPAN), :] = convolved(pre, taps, p).astype(BF16)
        return 0

    lax.fori_loop(0, step_out.shape[0], one, 0, unroll=16)


def mixer_kernel(inner_count, shared, z_count, place, taps, half, half_other, step, cum, other, *refs):
    pieces, refs = refs[:z_count], refs[z_count:]
    tail = 8 if shared else 9
    source, refs = refs[:-tail], refs[-tail:]
    if shared:
        tok, source = source[0], ()
        x_out, states_out, last_out, through_out, weight, pre, sems, wsems = refs
        source = (None,)
    else:
        x_out, states_out, last_out, through_out, tok, weight, pre, sems, wsems = refs
    span = (tok.shape[0] - HALO) // TEAM
    quarter, core = place[0], place[3]
    width = x_out.shape[1]
    parts = []
    for d, piece in enumerate(pieces):
        view = piece
        if piece.shape[1] != width:
            view = piece.at[:, pl.ds(pl.multiple_of(core * width, width), width)]
        parts += [(view, d, 0), (other.at[d], d, 1)]

    def keep(result, j):
        if j == 0:
            pre[pl.ds(0, HALO), :] = result[:HALO].astype(BF16)
            result = result[HALO:]
        whose = quarter ^ j
        pre[pl.ds(pl.multiple_of(HALO + whose * span, HALO), span), :] = result.astype(BF16)

    projected(place, source, parts, tok, weight, sems, wsems, inner_count, keep)
    heads = spread(width)

    def one(p, carry):
        state, log_sum = carry
        rows = pl.ds(pl.multiple_of(p * SPAN, SPAN), SPAN)
        x = convolved(pre, taps, p).astype(BF16)
        x_out[rows, :] = x
        states_out[p] = state
        cum_p = cum[p]
        ends = cum_p[:, SPAN - 1 :]
        to_end = jnp.exp(ends - cum_p) * step[p]
        scaled = (x.astype(F32) * over_lanes(to_end, heads)).astype(BF16)
        b = jnp.where(core == 0, half[rows, :], half_other[rows, :])
        fresh = lax.dot_general(b, scaled, (((0,), (0,)), ((), ())), preferred_element_type=F32)
        end_row = jnp.sum(ends * heads, axis=0, keepdims=True)
        return jnp.exp(end_row) * state + fresh, log_sum + end_row

    state, log_sum = lax.fori_loop(
        0, step.shape[0], one, (jnp.zeros((N, width), F32), jnp.zeros((1, width), F32)), unroll=16
    )
    last_out[...] = state.astype(BF16)
    through_out[...] = jnp.broadcast_to(jnp.exp(log_sum), through_out.shape)


def gate_kernel(inner_count, shared, z_count, place, *refs):
    pieces, refs = refs[:z_count], refs[z_count:]
    tail = 4 if shared else 5
    source, refs = refs[:-tail], refs[-tail:]
    if shared:
        tok = source[0]
        source = (None,)
        gate_out, weight, sems, wsems = refs
    else:
        gate_out, tok, weight, sems, wsems = refs
    span = (tok.shape[0] - HALO) // TEAM
    quarter = place[0]
    parts = []
    for d, piece in enumerate(pieces):
        rows = piece.shape[0] // 2
        parts += [(piece.at[pl.ds(m * rows, rows)], d, m) for m in range(2)]

    def keep(result, j):
        result = result[HALO:] if j == 0 else result
        gate_out[pl.ds(pl.multiple_of((quarter ^ j) * span, span), span), :] = result.astype(BF16)

    projected(place, source, parts, tok, weight, sems, wsems, inner_count, keep)


def scan_kernel(place, half, half_other, x_vals, gate, step, cum, states, prior, gated_out):
    width = x_vals.shape[1]
    heads_mine = width // P_SIZE
    heads = spread(width)
    core = place[3]
    lane = lax.broadcasted_iota(jnp.int32, (SPAN, width), 1) // P_SIZE
    row = lax.broadcasted_iota(jnp.int32, (SPAN, SPAN), 0)
    column = lax.broadcasted_iota(jnp.int32, (SPAN, SPAN), 1)
    lower = column <= row
    entering = prior[...].astype(F32)

    def one(p, before):
        rows = pl.ds(pl.multiple_of(p * SPAN, SPAN), SPAN)
        first, second = half[rows, :], half_other[rows, :]
        b = jnp.where(core == 0, first, second)
        c = jnp.where(core == 0, second, first)
        x = x_vals[rows, :]
        cum_p = cum[p]
        step_p = step[p]
        scores = lax.dot_general(
            c, b, (((1,), (1,)), ((), ())), preferred_element_type=F32
        )
        cum_t = cum_p.T
        mixes = []
        parts = []
        for h in range(heads_mine):
            spacing = jnp.where(lower, cum_t[:, h : h + 1] - cum_p[h : h + 1, :], -jnp.inf)
            mixes.append((scores * jnp.exp(spacing) * step_p[h : h + 1, :]).astype(BF16))
            parts.append(jnp.where(lane == h, x, jnp.zeros_like(x)))
        diagonal = wide_dot(jnp.concatenate(mixes, axis=1), jnp.concatenate(parts, axis=0))
        state = states[p] + jnp.exp(before) * entering
        decay = over_lanes(jnp.exp(cum_p), heads)
        y = diagonal + decay * wide_dot(c, state.astype(BF16))
        g = gate[rows, :].astype(F32)
        gated_out[rows, :] = (y * (g / (1.0 + jnp.exp(-g)))).astype(BF16)
        return before + jnp.sum(cum_p[:, SPAN - 1 :] * heads, axis=0, keepdims=True)

    lax.fori_loop(0, step.shape[0], one, jnp.zeros((1, width), F32), unroll=16)


def norm_kernel(inner_count, parts, gain, out):
    width = parts.shape[2]
    group_width = H * P_SIZE // G
    for g in range(G):
        members = []
        power = 0.0
        for c in range(g * group_width, (g + 1) * group_width, width):
            index = c // width
            i, k = index // TEAM, index % TEAM
            wide = parts[k * inner_count + i].astype(F32)
            members.append((c, wide))
            power = power + jnp.sum(wide * wide, axis=1, keepdims=True)
        scale = lax.rsqrt(power / group_width + EPSILON)
        for c, wide in members:
            out[:, c : c + width] = (wide * scale * gain[:, c : c + width]).astype(BF16)


def on_device(
    tokens,
    project_weight,
    state_weight,
    step_weight,
    mixer_taps,
    state_taps,
    step_bias,
    decay_log,
    norm_gain,
):
    ctx_count = lax.axis_size("ctx")
    inner_count = lax.axis_size("inner")
    z_count = ctx_count // 2
    members = TEAM * inner_count

    rows_here, _, width_here = project_weight.shape
    row_count, model_width = tokens.shape
    heads_here = step_weight.shape[1]
    heads_mine = heads_here // TEAM
    width_mine = width_here // TEAM
    per_group = H // G
    spread_out = heads_here // per_group, per_group // heads_here

    def at(kernel):
        return lambda *refs: kernel(here(*spread_out), *refs)

    total = members * row_count
    count = total // SPAN

    def sds(shape, dtype):
        return jax.ShapeDtypeStruct(shape, dtype)

    partner = swapped(tokens, "ctx", 2)
    near = inner_blocks(tokens, at, inner_count, ctx_count)
    beyond = inner_blocks(partner, at, inner_count, ctx_count)
    blocks = (
        near
        + [swapped(b, "ctx", 1) for b in near]
        + beyond
        + [swapped(b, "ctx", 1) for b in beyond]
    )
    tail = pl.pallas_call(
        at(tail_kernel),
        in_specs=[ANY] * (2 * inner_count),
        out_specs=VMEM,
        out_shape=sds((HALO, model_width), BF16),
        scratch_shapes=[pltpu.SemaphoreType.DMA],
        compiler_params=SMALL,
        name="tail",
    )(*blocks[: 2 * inner_count])
    halo = jnp.zeros_like(tail)
    for k in range(2):
        pairs = [
            (c - 2 + m, c + 2 * k + m) for c in range(TEAM, ctx_count, TEAM) for m in range(2)
        ]
        halo = halo + lax.ppermute(tail, "ctx", pairs)

    pair = 2 * width_mine
    slice_cols = state_weight.shape[2]
    chunks = 4
    x_sides = pl.pallas_call(
        at(mixer_columns_kernel),
        in_specs=[HBM],
        out_specs=[VMEM] * 2,
        out_shape=[sds((rows_here, pair), BF16)] * 2,
        scratch_shapes=[
            pltpu.VMEM((chunks, rows_here // chunks, 2, width_here), BF16),
            pltpu.SemaphoreType.DMA((chunks,)),
        ],
        compiler_params=SMALL,
        name="columns",
    )(project_weight)

    def held_in_vmem(values):
        return [pltpu.VMEM(v.shape, v.dtype) for v in values] + [pltpu.SemaphoreType.DMA((len(values),))]

    to_prepare = (state_weight, step_weight.T)
    state_turned, *step_sides = pl.pallas_call(
        at(prepare_kernel),
        in_specs=[HBM] * 2,
        out_specs=[VMEM] * 3,
        out_shape=[
            sds((2 * slice_cols, rows_here), BF16),
            sds((PAD, rows_here), BF16),
            sds((PAD, rows_here), BF16),
        ],
        scratch_shapes=held_in_vmem(to_prepare),
        compiler_params=SMALL,
        name="prepare",
    )(*to_prepare)
    to_set = (
        project_weight,
        state_taps,
        mixer_taps,
        step_bias.reshape(1, -1),
        decay_log.reshape(1, -1),
    )
    settings = pl.pallas_call(
        at(functools.partial(settings_kernel, heads_mine)),
        in_specs=[HBM] * 5,
        out_specs=[VMEM] * 7,
        out_shape=[
            sds((rows_here, width_mine), BF16),
            sds((rows_here, width_mine), BF16),
            sds((rows_here, pair), BF16),
            sds((PAD, N), F32),
            sds((PAD, width_mine), F32),
            sds((PAD, SPAN), F32),
            sds((PAD, SPAN), F32),
        ],
        scratch_shapes=held_in_vmem(to_set),
        compiler_params=SMALL,
        name="settings",
    )(*to_set)
    gate_mine, gate_sent = settings[:2], settings[2]

    x_pieces = gathered_rows(lambda d: x_sides[d % 2], z_count)

    def of_core(piece, which):
        return lax.dynamic_slice_in_dim(piece, which * width_mine, width_mine, 1)

    x_sent = pl.pallas_call(
        at(partner_columns_kernel),
        in_specs=[VMEM] * z_count,
        out_specs=VMEM,
        out_shape=sds((z_count, rows_here, width_mine), BF16),
        compiler_params=SMALL,
        name="xsplit",
    )(*x_pieces)
    x_other = swapped(x_sent, "ctx", 1)
    if width_mine % LANES:
        x_pieces = [of_core(p, lax.axis_index("ctx") % 2) for p in x_pieces]

    part_rows = 2 * slice_cols // G
    if part_rows % (2 * HALO) == 0:
        sent = pl.pallas_call(
            at(functools.partial(sent_kernel, lambda j: group_of(j, *spread_out))),
            in_specs=[VMEM],
            out_specs=[VMEM] * (inner_count - 1),
            out_shape=[sds((part_rows, rows_here), BF16)] * (inner_count - 1),
            compiler_params=SMALL,
            name="sent",
        )(state_turned)
        received = [swapped(sent[d - 1], "inner", d) for d in range(1, inner_count)]
        payload_call = pl.pallas_call(
            at(payload_kernel),
            in_specs=[VMEM] * (inner_count + 2),
            out_specs=[VMEM] * 2,
            out_shape=[sds((2 * N + PAD, rows_here), BF16)] * 2,
            compiler_params=SMALL,
            name="payload",
        )
        payloads = payload_call(state_turned, *received, *step_sides)
    else:
        to_each = jnp.concatenate(
            [
                lax.slice_in_dim(state_turned, g * part_rows, (g + 1) * part_rows, axis=0)
                for g in [(j * heads_here) // per_group for j in range(inner_count)]
            ],
            axis=0,
        ).reshape(inner_count, part_rows, rows_here)
        state_rows = lax.all_to_all(to_each, "inner", 0, 0, tiled=True)
        state_rows = state_rows.reshape(inner_count, 2, part_rows // 2, rows_here)
        state_rows = state_rows.transpose(1, 0, 2, 3).reshape(2 * N, rows_here)
        payloads = [jnp.concatenate([state_rows, s], axis=0) for s in step_sides]
    state_pieces = gathered_rows(lambda d: payloads[d % 2], z_count)
    state_sent = pl.pallas_call(
        at(partner_rows_kernel),
        in_specs=[VMEM] * z_count,
        out_specs=VMEM,
        out_shape=sds((z_count, N + PAD, rows_here), BF16),
        compiler_params=SMALL,
        name="ssplit",
    )(*state_pieces)
    state_other = swapped(state_sent, "ctx", 1)
    state_matrix = pl.pallas_call(
        at(functools.partial(assemble_kernel, heads_mine)),
        in_specs=[VMEM] * (1 + z_count),
        out_specs=VMEM,
        out_shape=sds((model_width, N + LANES), BF16),
        compiler_params=SMALL,
        name="assemble",
    )(state_other, *state_pieces)

    gate_other = swapped(gate_sent, "ctx", 1)
    gate_chip = [
        jnp.concatenate([gate_mine[s], gate_other[:, s * width_mine : (s + 1) * width_mine]], axis=0)
        for s in range(2)
    ]
    gate_pieces = gathered_rows(lambda d: gate_chip[d % 2], z_count)

    taps_state, taps_mine, bias_mine, rate_mine = settings[3:]

    shared = total * model_width <= 2**23
    tok_shape = (HALO + total, model_width)
    held = 2 * tok_shape[0] * model_width
    limit = pltpu.CompilerParams(vmem_limit_bytes=min(60 << 20, held + (4 << 20 if shared else 22 << 20)))

    def scratch(width, pre_width, own_tok):
        made = [pltpu.VMEM(tok_shape, BF16)] if own_tok else []
        if width:
            made.append(pltpu.VMEM((model_width, width), BF16))
        if pre_width:
            made.append(pltpu.VMEM((HALO + total, pre_width), BF16))
        return made + [pltpu.SemaphoreType.DMA((members + 1,)), pltpu.SemaphoreType.DMA((2 * z_count,))]

    source = list(blocks) + [halo]
    any_of = lambda values: [ANY] * len(values)
    state_outs = [sds((total, N), BF16), sds((count, PAD, SPAN), F32), sds((count, PAD, SPAN), F32)]
    outs = pl.pallas_call(
        at(functools.partial(state_kernel, inner_count)),
        in_specs=[VMEM] * 4 + any_of(source),
        out_specs=[VMEM] * (4 if shared else 3),
        out_shape=state_outs + ([sds(tok_shape, BF16)] if shared else []),
        scratch_shapes=scratch(0, N, not shared)[:-1],
        compiler_params=limit,
        name="state",
    )(taps_state, bias_mine, rate_mine, state_matrix, *source)
    half, step, cum = outs[:3]
    if shared:
        source = [outs[3]]
    held_spec = [VMEM] if shared else any_of(source)
    half_other = swapped(half, "ctx", 1)

    x_vals, states, last_state, through = pl.pallas_call(
        at(functools.partial(mixer_kernel, inner_count, shared, z_count)),
        in_specs=[VMEM] * 5 + [ANY] + any_of(x_pieces) + held_spec,
        out_specs=[VMEM, VMEM, VMEM, VMEM],
        out_shape=[
            sds((total, width_mine), BF16),
            sds((count, N, width_mine), F32),
            sds((N, width_mine), BF16),
            sds((PAD, width_mine), F32),
        ],
        scratch_shapes=scratch(width_mine, width_mine, not shared),
        compiler_params=limit,
        name="mixer",
    )(taps_mine, half, half_other, step, cum, x_other, *x_pieces, *source)

    hops = ctx_count // TEAM - 1
    pairs = [(c, c + TEAM) for c in range(ctx_count - TEAM)]
    prior = jnp.zeros_like(last_state)
    for hop in range(hops):
        sent = last_state
        if hop:
            sent = (through[:1] * prior.astype(F32) + last_state.astype(F32)).astype(BF16)
        prior = lax.ppermute(sent, "ctx", pairs)

    gate_values = pl.pallas_call(
        at(functools.partial(gate_kernel, inner_count, shared, z_count)),
        in_specs=any_of(gate_pieces) + held_spec,
        out_specs=VMEM,
        out_shape=sds((total, width_mine), BF16),
        scratch_shapes=scratch(width_mine, 0, not shared),
        compiler_params=limit,
        name="gate",
    )(*gate_pieces, *source)

    gated = pl.pallas_call(
        at(scan_kernel),
        in_specs=[VMEM] * 8,
        out_specs=VMEM,
        out_shape=sds((total, width_mine), BF16),
        compiler_params=limit,
        name="scan",
    )(half, half_other, x_vals, gate_values, step, cum, states, prior)

    teams = [[t * members + m for m in range(members)] for t in range(ctx_count // TEAM)]
    parts = lax.all_to_all(
        gated, ("ctx", "inner"), 0, 0, axis_index_groups=teams, tiled=True
    ).reshape(members, row_count, width_mine)
    return pl.pallas_call(
        lambda *refs: norm_kernel(inner_count, *refs),
        in_specs=[VMEM, VMEM],
        out_specs=VMEM,
        out_shape=sds((row_count, H * P_SIZE), BF16),
        compiler_params=limit,
        name="norm",
    )(parts, norm_gain.reshape(1, -1))


def solution(mesh):
    placed = (
        P(("ctx", "inner"), None),
        P("ctx", None, "inner"),
        P("ctx", None, "inner"),
        P("ctx", "inner"),
        P(None, "inner"),
        P(),
        P("inner"),
        P("inner"),
        P(),
    )

    return jax.shard_map(
        on_device, mesh=mesh, in_specs=placed, out_specs=P(("ctx", "inner"), None), check_vma=False
    )
```
